128 devices in a mesh: seq: 8 (over z, core), grp: 16 (over x, y).
Axes of the slice: x: 4, y: 4, z: 4, core: 2. Of those that a mesh axis runs over, the one named last changes fastest.
Arguments:
- qkv: bfloat16 [16384, 3, 2048], P(('seq', 'grp')), may hold values from -6 to 6
- cluster_lists: int32 [16, 16, 1024], P('seq', 'grp'), may hold values from 0 to 16383, as said below
- w_out: bfloat16 [2048, 2048], replicated, may hold values from -0.125 to 0.125
- norm_gain: bfloat16 [2048], replicated, may hold values from 0.099609375 to 1.8984375
- router: bfloat16 [2048, 128], replicated, may hold values from -0.125 to 0.125
- expert_lists: int32 [128, 512], replicated, may hold values from 0 to 16383, as said below
- w_gate: bfloat16 [128, 2048, 768], P(('seq', 'grp')), may hold values from -0.125 to 0.125
- w_up: bfloat16 [128, 2048, 768], P(('seq', 'grp')), may hold values from -0.125 to 0.125
- w_down: bfloat16 [128, 768, 2048], P(('seq', 'grp')), may hold values from -0.21875 to 0.21875
Outputs:
- layer_out: bfloat16 [16384, 2048], P(('seq', 'grp'))
The draws below stay inside these ranges and needn't reach their ends.
Inputs may be any that keep to these rules, and one draw needn't show every extreme that they name: `cluster_lists`: within each head the 16 lists are disjoint, each ascending, and together hold every one of the 16384 tokens once. Of the 128 tokens of an aligned block, one list holds at most 12, and for every head some list holds exactly 12. `expert_lists`: each list is ascending with distinct rows. Of the 128 rows of an aligned block, one list holds at most 6, and some list holds exactly 6.
All inputs are finite; a program needn't handle non-finite values.
Results may differ from the reference program's by a relative error of at most 0.019.
Values may be sent and summed in bfloat16 or wider, within the bound.
No kernel may reach another device: no remote copies, remote signals or barrier semaphores. Data moves between devices by JAX's collectives and lax.ppermute only.
A program may use at most 128 MiB of HBM per device.

```python
import jax
import jax.numpy as jnp
from jax import lax

HEADS = 16
HEAD_DIM = 128
D = 2048
EXPERT_HIDDEN = 768
ECHOOSE = 512
C = 1024
CLUSTERS = 16
TOKENS = 16384
ROWS = 128
HD = 2048
EXPERTS = 128


def draw_qkv(key, part):
    values = jnp.clip(jax.random.normal(key, (TOKENS, 3, HEADS * HEAD_DIM), jnp.float32), -4.0, 4.0)
    return values.astype(jnp.bfloat16)


def draw_cluster_lists(key, part):
    blocks = TOKENS // ROWS
    mean_load = ROWS // CLUSTERS

    def one_head(head_key):
        key_shift, key_heavy, key_mix = jax.random.split(head_key, 3)
        loads_base = jnp.where(jnp.arange(CLUSTERS, dtype=jnp.int32) < CLUSTERS // 2, mean_load // 2, 3 * mean_load // 2)
        loads_base = jax.random.permutation(key_heavy, loads_base)
        shifts = jax.random.permutation(key_shift, blocks) % CLUSTERS
        counts = loads_base[(jnp.arange(CLUSTERS, dtype=jnp.int32)[None, :] + shifts[:, None]) % CLUSTERS]
        bounds = jnp.cumsum(counts, axis=1)
        offsets = jnp.arange(ROWS, dtype=jnp.int32)
        labels = jnp.sum((offsets[None, :, None] >= bounds[:, None, :]).astype(jnp.int32), axis=2)
        labels = jax.random.permutation(key_mix, labels, axis=1, independent=True)
        assign = labels.reshape(TOKENS)
        order = jnp.argsort(assign * TOKENS + jnp.arange(TOKENS, dtype=jnp.int32), stable=True)
        return order.reshape(CLUSTERS, C).astype(jnp.int32)
    return jax.vmap(one_head)(jax.random.split(jax.random.fold_in(key, 11), HEADS))


def draw_expert_lists(key, part):
    blocks = TOKENS // ROWS
    mean_load = ECHOOSE // EXPERTS
    key_heavy, key_shift, key_pick = jax.random.split(jax.random.fold_in(key, 13), 3)
    loads_base = jnp.where(jnp.arange(EXPERTS, dtype=jnp.int32) < EXPERTS // 2, mean_load // 2, 3 * mean_load // 2)
    loads_base = jax.random.permutation(key_heavy, loads_base)
    shifts = jax.random.permutation(key_shift, blocks)
    counts = loads_base[(jnp.arange(EXPERTS, dtype=jnp.int32)[None, :] + shifts[:, None]) % EXPERTS]
    ranks = jnp.broadcast_to(jnp.arange(ROWS, dtype=jnp.int32), (EXPERTS, blocks, ROWS))
    ranks = jax.random.permutation(key_pick, ranks, axis=2, independent=True)
    chosen = (ranks < counts.T[:, :, None]).reshape(EXPERTS, TOKENS)
    order_key = jnp.where(chosen, 0, 1) * TOKENS + jnp.arange(TOKENS, dtype=jnp.int32)[None, :]
    order = jnp.argsort(order_key, axis=1, stable=True)
    return order[:, :ECHOOSE].astype(jnp.int32)


def steps_of(stream_key, shape, cuts, smallest, high):
    loudness = 1.0
    for position, shards_of in cuts:
        steps = jax.random.uniform(jax.random.fold_in(jax.random.fold_in(stream_key, 6), position), (shards_of,), jnp.float32, smallest / len(cuts), high / len(cuts))
        loudness = loudness * jnp.repeat(jnp.exp(steps), shape[position] // shards_of).reshape((-1,) + (1,) * (len(shape) - 1 - position))
    return loudness


def bell_draw(own_key, dims, spread, bound, pieces=(), kind=jnp.bfloat16):
    drawn = spread * jax.random.normal(own_key, dims, jnp.float32)
    if pieces:
        drawn = drawn * steps_of(own_key, dims, pieces, -0.22, 0.18)
    return jnp.clip(drawn, -bound, bound).astype(kind)


def setup_inputs(seed: int = 0) -> dict:
    key_list = jax.random.split(jax.random.key(seed), 10)
    return {
        "qkv": draw_qkv(jax.random.fold_in(key_list[9], 71), 0),
        "cluster_lists": draw_cluster_lists(jax.random.fold_in(key_list[9], 71), 0),
        "w_out": bell_draw(key_list[2], (HD, D), HD ** -0.5, 0.125),
        "norm_gain": jnp.clip(1.0 + 0.18 * jax.random.normal(key_list[3], (D,), jnp.float32), 0.099609375, 1.8984375).astype(jnp.bfloat16),
        "router": bell_draw(key_list[4], (D, EXPERTS), D ** -0.5, 0.125),
        "expert_lists": draw_expert_lists(jax.random.fold_in(key_list[9], 71), 0),
        "w_gate": bell_draw(key_list[6], (EXPERTS, D, EXPERT_HIDDEN), D ** -0.5, 0.125, ((0, 128),)),
        "w_up": bell_draw(key_list[7], (EXPERTS, D, EXPERT_HIDDEN), D ** -0.5, 0.125, ((0, 128),)),
        "w_down": bell_draw(key_list[8], (EXPERTS, EXPERT_HIDDEN, D), EXPERT_HIDDEN ** -0.5, 0.21875, ((0, 128),)),
    }


def cluster_attention(packed):
    queries = packed[:, 0, :]
    keys_all = packed[:, 1, :]
    values_all = packed[:, 2, :]
    scores = jnp.dot(queries, keys_all.T, preferred_element_type=jnp.float32) * HEAD_DIM ** (-0.5)
    positions = jnp.arange(C, dtype=jnp.int32)
    allowed = positions[:, None] >= positions[None, :]
    scores = jnp.where(allowed, scores, -jnp.inf)
    top_score = lax.optimization_barrier(jnp.max(scores, axis=1, keepdims=True))
    exp_scores = jnp.exp(scores - top_score)
    weights = exp_scores.astype(jnp.bfloat16)
    totals = lax.optimization_barrier(jnp.sum(exp_scores, axis=1, keepdims=True))
    return (jnp.dot(weights, values_all, preferred_element_type=jnp.float32) / totals).astype(jnp.bfloat16)

def reference(qkv, cluster_lists, w_out, norm_gain, router, expert_lists, w_gate, w_up, w_down):
    by_head = qkv.reshape(TOKENS, 3, HEADS, HEAD_DIM).transpose(2, 0, 1, 3)

    def one_head(operands):
        head_rows, head_lists = operands

        def one_cluster(members):
            return cluster_attention(head_rows[members])
        outputs = lax.map(one_cluster, head_lists)
        empty = jnp.zeros((TOKENS, HEAD_DIM), jnp.bfloat16)
        return empty.at[head_lists.reshape(-1)].add(outputs.reshape(-1, HEAD_DIM))
    attended = lax.map(one_head, (by_head, cluster_lists))
    attended = attended.transpose(1, 0, 2).reshape(TOKENS, HEADS * HEAD_DIM)
    mixed = jnp.dot(attended, w_out, preferred_element_type=jnp.float32).astype(jnp.bfloat16)
    wide = mixed.astype(jnp.float32)
    mean_square = lax.optimization_barrier(jnp.mean(wide * wide, axis=1, keepdims=True))
    normed = (wide * lax.rsqrt(mean_square + 1e-06) * norm_gain.astype(jnp.float32)).astype(jnp.bfloat16)
    gates = jax.nn.sigmoid(jnp.dot(normed, router, preferred_element_type=jnp.float32))

    def one_expert(operands):
        chosen, gate_w, up_w, down_w = operands
        rows_in = normed[chosen]
        gate_part = jnp.dot(rows_in, gate_w, preferred_element_type=jnp.float32)
        up_part = jnp.dot(rows_in, up_w, preferred_element_type=jnp.float32)
        hidden = (jax.nn.silu(gate_part) * up_part).astype(jnp.bfloat16)
        return jnp.dot(hidden, down_w, preferred_element_type=jnp.float32).astype(jnp.bfloat16)
    results = lax.map(one_expert, (expert_lists, w_gate, w_up, w_down))
    expert_ids = jnp.arange(EXPERTS, dtype=jnp.int32)[:, None]
    weights = gates[expert_lists, expert_ids]
    terms = (weights[:, :, None] * results.astype(jnp.float32)).reshape(-1, D)
    combined = jnp.zeros((TOKENS, D), jnp.float32).at[expert_lists.reshape(-1)].add(terms)
    return (wide + combined).astype(jnp.bfloat16)
```

```python
import jax
import jax.numpy as jnp
from jax import lax
from jax.experimental import pallas as pl
from jax.experimental.pallas import tpu as pltpu
from jax.sharding import PartitionSpec as P

BF16 = jnp.bfloat16
F32 = jnp.float32
I32 = jnp.int32
ALL = ("seq", "grp")

SEQ = 8
GRP = 16
DEVICES = 128
ROWS = 128
HEAD = 128
WIDTH = 2048
CHUNKS = WIDTH // 128
CLUSTER = 1024
SLOTS = 12
LOW = 8
HIGH = 4
ESLOTS = 6
CHOSEN = 512
HIDDEN = 768
SENT = DEVICES * ESLOTS
GROUP = 32
GROWS = GROUP * SLOTS
PLACES = DEVICES * SLOTS

NN = (((1,), (0,)), ((), ()))
NT = (((1,), (1,)), ((), ()))
TN = (((0,), (0,)), ((), ()))
VMEM_LIMIT = 60 * 1024 * 1024


def iota(shape, axis):
    return lax.broadcasted_iota(I32, shape, axis)


def dot(a, b, dims=NN):
    return lax.dot_general(a, b, dims, preferred_element_type=F32)


def whole(space=pltpu.VMEM):
    return pl.BlockSpec(memory_space=space)


def rank_in_block(block, most):
    lane = iota(block.shape, 1)
    rank = jnp.zeros(block.shape, I32)
    for back in range(1, most):
        same = (pltpu.roll(block, back, 1) == block) & (lane >= back)
        rank = rank + jnp.where(same, 1, 0)
    return rank


def request_kernel(place_ref, lists_ref, out_ref):
    grp = place_ref[1]
    line = iota((128, CLUSTER), 0)
    high = jnp.zeros((DEVICES, 128), F32)
    for h in range(2):
        token = lists_ref[h]
        block = token >> 7
        rank = rank_in_block(block, SLOTS)
        row = ((token & 127) + 1).astype(F32)
        member = jnp.where(block == line, 1.0, 0.0).astype(BF16)
        low_line = jnp.where(rank < LOW, grp * LOW + rank, -1)
        high_line = jnp.where(rank < LOW, -1, grp * LOW + HIGH * h + rank - LOW)
        low_rows = jnp.where(low_line == line, row, 0.0).astype(BF16)
        high_rows = jnp.where(high_line == line, row, 0.0).astype(BF16)
        out_ref[:, h, :] = dot(member, low_rows, NT)
        high = high + dot(member, high_rows, NT)
    out_ref[:, 2, :] = high
    out_ref[:, 3, :] = jnp.zeros((DEVICES, 128), F32)


def place_order(index):
    group = index // GROWS
    inner = index - group * GROWS
    upper = inner - GROUP * LOW
    is_low = inner < GROUP * LOW
    source = group * GROUP + jnp.where(is_low, inner >> 3, upper >> 2)
    slot = jnp.where(is_low, inner & 7, LOW + (upper & 3))
    return source, slot


def order_kernel(lists_ref, out_ref):
    line = iota((128, CLUSTER), 0)
    source, slot = place_order(iota((1, PLACES), 1))
    spread = jnp.where(iota((128, PLACES), 0) == source, 1.0, 0.0).astype(BF16)
    key = (source * SLOTS + slot).astype(F32)
    for h in range(2):
        member = jnp.where((lists_ref[h] >> 7) == line, 1.0, 0.0).astype(BF16)
        count = dot(jnp.ones((8, CLUSTER), BF16), member, NT)
        held = dot(count.astype(BF16), spread)
        out_ref[h] = jnp.where(slot.astype(F32) < held, key, 1e9)


def expert_index_kernel(place_ref, lists_ref, rows_ref, slots_ref):
    me = place_ref[0]
    lists = lists_ref[...]
    inside = (lists >> 7) == me
    position = iota((DEVICES, CHOSEN), 1)
    before = jnp.sum(jnp.where(lists < me * ROWS, 1.0, 0.0), axis=1, keepdims=True).astype(I32)
    row = (lists - me * ROWS + 1).astype(F32)
    rank = jnp.where(inside, position - before, -1)
    lane = iota((DEVICES, 128), 1)
    rows = jnp.zeros((DEVICES, 128), F32)
    for k in range(ESLOTS):
        found = jnp.sum(jnp.where(rank == k, row, 0.0), axis=1, keepdims=True)
        rows = jnp.where(lane == k, found, rows)
    rows_ref[...] = rows.astype(I32)
    mine = lists_ref[pl.ds(me, 1), :]
    block = mine >> 7
    slots_ref[...] = block * ESLOTS + rank_in_block(block, ESLOTS)


def select_kernel(request_ref, qkv_ref, out_ref):
    rows = jnp.sum(request_ref[...], axis=0)
    token = (iota((ROWS, 128), 0) + 1).astype(F32)
    lane_head = (iota((ROWS, 128), 1) >> 2) & 1
    high_match = rows[2:3, :] == token
    high = jnp.zeros((128, 3 * HEAD), F32)
    for h in range(2):
        columns = slice(h * HEAD, (h + 1) * HEAD)
        packed = jnp.concatenate([qkv_ref[c, :, columns] for c in range(3)], axis=1)
        low_match = jnp.where(rows[h : h + 1, :] == token, 1.0, 0.0).astype(BF16)
        low = dot(low_match, packed, TN).astype(BF16)
        mine = jnp.where(high_match & (lane_head == h), 1.0, 0.0).astype(BF16)
        high = high + dot(mine, packed, TN)
        for c in range(3):
            out_ref[:, h * 3 + c] = low[:, c * HEAD : (c + 1) * HEAD].reshape(GRP, 8, HEAD)
    high = high.astype(BF16)
    for c in range(3):
        out_ref[:, 6 + c] = high[:, c * HEAD : (c + 1) * HEAD].reshape(GRP, 8, HEAD)


def attend_kernel(order_ref, x_ref, out_ref, packed_ref):
    scale = HEAD ** (-0.5)
    low_rows = GROUP * LOW
    high_rows = GROUP * HIGH
    joint = iota((2 * high_rows, high_rows), 0)
    apart = iota((2 * high_rows, high_rows), 1)
    same_place = (joint >> 3) * HIGH + (joint & 3) == apart
    spread = [
        jnp.where(same_place & (((joint >> 2) & 1) == h), 1.0, 0.0).astype(BF16) for h in range(2)
    ]
    groups = DEVICES // GROUP
    for i in range(groups):
        blocks = slice(i * GROUP, (i + 1) * GROUP)
        for c in range(3):
            both = x_ref[blocks, 6 + c].reshape(2 * high_rows, HEAD)
            for h in range(2):
                start = i * GROWS
                packed_ref[h, c, start : start + low_rows, :] = x_ref[blocks, h * 3 + c].reshape(
                    low_rows, HEAD
                )
                packed_ref[h, c, start + low_rows : start + GROWS, :] = dot(
                    spread[h], both, TN
                ).astype(BF16)
    for i in range(groups):
        blocks = slice(i * GROUP, (i + 1) * GROUP)
        seen = (i + 1) * GROWS
        source, slot = place_order(i * GROWS + iota((GROWS, 1), 0))
        query_order = (source * SLOTS + slot).astype(F32)
        joined = jnp.zeros((2 * high_rows, HEAD), F32)
        for h in range(2):
            queries = packed_ref[h, 0, i * GROWS : seen, :]
            scores = dot(queries, packed_ref[h, 1, :seen, :], NT) * scale
            key_order = order_ref[h, 0:1, :seen]
            scores = jnp.where(key_order <= query_order, scores, -1e30)
            top = jnp.max(scores, axis=1, keepdims=True)
            grown = jnp.exp(scores - top)
            totals = jnp.sum(grown, axis=1, keepdims=True)
            summed = dot(grown.astype(BF16), packed_ref[h, 2, :seen, :])
            result = (summed / totals).astype(BF16)
            out_ref[blocks, h] = result[:low_rows].reshape(GROUP, 8, HEAD)
            joined = joined + dot(spread[h], result[low_rows:])
        out_ref[blocks, 2] = joined.astype(BF16).reshape(GROUP, 8, HEAD)


def mix_kernel(
    rows_ref, request_ref, came_ref, w_out_ref, gain_ref, mixed_ref, out_ref, w_ref, att_ref, tall_ref, tile_ref, sems
):
    parts = sems.shape[0]
    depth = WIDTH // parts
    copies = [
        pltpu.make_async_copy(
            w_out_ref.at[pl.ds(p * depth, depth), :], w_ref.at[pl.ds(p * depth, depth), :], sems.at[p]
        )
        for p in range(parts)
    ]
    for copy in copies:
        copy.start()
    token = (iota((ROWS, 128), 0) + 1).astype(F32)
    lane_head = (iota((ROWS, 128), 1) >> 2) & 1
    for s in range(SEQ):
        peers = slice(s * GRP, (s + 1) * GRP)
        rows = jnp.sum(request_ref[peers], axis=0)
        high_match = rows[2:3, :] == token
        high = came_ref[peers, 2].reshape(128, HEAD)
        for h in range(2):
            low_match = jnp.where(rows[h : h + 1, :] == token, 1.0, 0.0).astype(BF16)
            mine = jnp.where(high_match & (lane_head == h), 1.0, 0.0).astype(BF16)
            got = dot(low_match, came_ref[peers, h].reshape(128, HEAD)) + dot(mine, high)
            start = (2 * s + h) * HEAD
            att_ref[:, start : start + HEAD] = got.astype(BF16)
    total = jnp.zeros((ROWS, WIDTH), F32)
    for p in range(parts):
        copies[p].wait()
        total = total + dot(
            att_ref[:, p * depth : (p + 1) * depth], w_ref[p * depth : (p + 1) * depth, :]
        )
    mixed = total.astype(BF16)
    mixed_ref[...] = mixed
    wide = mixed.astype(F32)
    mean_square = jnp.mean(wide * wide, axis=1, keepdims=True)
    normed = wide * lax.rsqrt(mean_square + 1e-06) * gain_ref[...].astype(F32)
    for j in range(CHUNKS):
        tall_ref[pl.ds(j, ROWS, stride=CHUNKS), :] = normed[:, j * 128 : (j + 1) * 128]
    tile_ref[...] = tall_ref[...].astype(BF16).reshape(ROWS, CHUNKS, 128)

    def send(e, carry):
        for k in range(ESLOTS):
            out_ref[e * ESLOTS + k] = tile_ref[jnp.maximum(rows_ref[e, k] - 1, 0)]
        return carry

    lax.fori_loop(0, DEVICES, send, 0)


def expert_kernel(
    place_ref, slots_ref, x_ref, gate_hbm, up_hbm, down_hbm, router_ref, out_ref,
    gate_ref, up_ref, down_ref, tall_ref, rows_ref, sems,
):
    copies = [
        pltpu.make_async_copy(source.at[0], target, sems.at[n])
        for n, (source, target) in enumerate(
            [(gate_hbm, gate_ref), (up_hbm, up_ref), (down_hbm, down_ref)]
        )
    ]
    for copy in copies:
        copy.start()
    half = rows_ref.shape[0]
    me = place_ref[0]
    for part in range(CHOSEN // half):
        base = part * half

        def take(i, carry):
            for n in range(8):
                at = i * 8 + n
                tall_ref[pl.ds(pl.multiple_of(at * CHUNKS, CHUNKS), CHUNKS), :] = x_ref[
                    slots_ref[0, base + at]
                ].astype(F32)
            return carry

        lax.fori_loop(0, half // 8, take, 0)
        for j in range(CHUNKS):
            rows_ref[:, j * 128 : (j + 1) * 128] = tall_ref[pl.ds(j, half, stride=CHUNKS), :].astype(BF16)
        rows = rows_ref[...]
        logits = dot(rows, router_ref[...])
        mine = jnp.where(iota((half, 128), 1) == me, logits, 0.0)
        weight = jax.nn.sigmoid(jnp.sum(mine, axis=1, keepdims=True))
        if part == 0:
            copies[0].wait()
        gate = dot(rows, gate_ref[...])
        if part == 0:
            copies[1].wait()
        up = dot(rows, up_ref[...])
        hidden = (jax.nn.silu(gate) * up).astype(BF16)
        if part == 0:
            copies[2].wait()
        result = dot(hidden, down_ref[...]) * weight
        for j in range(CHUNKS):
            tall_ref[pl.ds(j, half, stride=CHUNKS), :] = result[:, j * 128 : (j + 1) * 128]

        def put(i, carry):
            for n in range(8):
                at = i * 8 + n
                out_ref[slots_ref[0, base + at]] = tall_ref[
                    pl.ds(pl.multiple_of(at * CHUNKS, CHUNKS), CHUNKS), :
                ].astype(BF16)
            return carry

        lax.fori_loop(0, half // 8, put, 0)


def combine_kernel(rows_ref, mixed_ref, x_ref, out_ref, tall_ref, flat_ref):
    token = iota((DEVICES, ROWS), 1) + 1
    total = mixed_ref[...].astype(F32)
    for k in range(ESLOTS):

        def take(i, carry):
            for n in range(8):
                e = i * 8 + n
                tall_ref[pl.ds(pl.multiple_of(e * CHUNKS, CHUNKS), CHUNKS), :] = x_ref[
                    e * ESLOTS + k
                ].astype(F32)
            return carry

        lax.fori_loop(0, DEVICES // 8, take, 0)
        for j in range(CHUNKS):
            flat_ref[:, j * 128 : (j + 1) * 128] = tall_ref[
                pl.ds(j, DEVICES, stride=CHUNKS), :
            ].astype(BF16)
        held = rows_ref[:, k : k + 1]
        kept = jnp.where(held > 0, flat_ref[...].astype(F32), 0.0).astype(BF16)
        match = jnp.where(held == token, 1.0, 0.0).astype(BF16)
        total = total + dot(match, kept, TN)
    out_ref[...] = total.astype(BF16)


def call(kernel, out_shape, in_specs, scratch=(), **kwargs):
    return pl.pallas_call(
        kernel,
        out_shape=out_shape,
        in_specs=in_specs,
        out_specs=jax.tree.map(lambda _: whole(), out_shape),
        scratch_shapes=list(scratch),
        compiler_params=pltpu.CompilerParams(vmem_limit_bytes=VMEM_LIMIT),
        **kwargs,
    )


def shape(dims, dtype=BF16):
    return jax.ShapeDtypeStruct(dims, dtype)


def exchange(array):
    return lax.all_to_all(array, ALL, split_axis=0, concat_axis=0, tiled=True)


def shards(qkv, cluster_lists, w_out, norm_gain, router, expert_lists, w_gate, w_up, w_down):
    grp = lax.axis_index("grp")
    place = jnp.stack([lax.axis_index("seq") * GRP + grp, grp]).astype(I32)
    smem = whole(pltpu.SMEM)
    hbm = whole(pl.ANY)

    request = call(request_kernel, shape((DEVICES, 4, 128), F32), [smem, whole()])(place, cluster_lists)
    asked = exchange(request)
    order = call(order_kernel, shape((2, 8, PLACES), F32), [whole()])(cluster_lists)
    rows, slots = call(
        expert_index_kernel,
        (shape((DEVICES, 128), I32), shape((1, CHOSEN), I32)),
        [smem, whole()],
    )(place, expert_lists)

    picked = pl.pallas_call(
        select_kernel,
        out_shape=shape((DEVICES, 9, 8, HEAD)),
        grid=(SEQ,),
        in_specs=[
            pl.BlockSpec((GRP, 4, 128), lambda s: (s, 0, 0)),
            pl.BlockSpec((3, ROWS, 2 * HEAD), lambda s: (0, 0, s)),
        ],
        out_specs=pl.BlockSpec((GRP, 9, 8, HEAD), lambda s: (s, 0, 0, 0)),
    )(asked, qkv.transpose(1, 0, 2))
    arrived = exchange(picked)

    outputs = call(
        attend_kernel,
        shape((DEVICES, 3, 8, HEAD)),
        [whole(), whole()],
        [pltpu.VMEM((2, 3, PLACES, HEAD), BF16)],
    )(order, arrived)
    came_back = exchange(outputs)

    mixed, outgoing = call(
        mix_kernel,
        (shape((ROWS, WIDTH)), shape((SENT, CHUNKS, 128))),
        [smem, whole(), whole(), hbm, whole()],
        [
            pltpu.VMEM((WIDTH, WIDTH), BF16),
            pltpu.VMEM((ROWS, WIDTH), BF16),
            pltpu.VMEM((ROWS * CHUNKS, 128), F32),
            pltpu.VMEM((ROWS, CHUNKS, 128), BF16),
            pltpu.SemaphoreType.DMA((4,)),
        ],
    )(rows, asked, came_back, w_out, norm_gain.reshape(1, WIDTH))
    incoming = exchange(outgoing)

    half = CHOSEN // 2
    produced = call(
        expert_kernel,
        shape((SENT, CHUNKS, 128)),
        [smem, smem, whole(), hbm, hbm, hbm, whole()],
        [
            pltpu.VMEM((WIDTH, HIDDEN), BF16),
            pltpu.VMEM((WIDTH, HIDDEN), BF16),
            pltpu.VMEM((HIDDEN, WIDTH), BF16),
            pltpu.VMEM((half * CHUNKS, 128), F32),
            pltpu.VMEM((half, WIDTH), BF16),
            pltpu.SemaphoreType.DMA((3,)),
        ],
    )(place, slots, incoming, w_gate, w_up, w_down, router)
    results = exchange(produced)

    return call(
        combine_kernel,
        shape((ROWS, WIDTH)),
        [whole(), whole(), whole()],
        [pltpu.VMEM((DEVICES * CHUNKS, 128), F32), pltpu.VMEM((DEVICES, WIDTH), BF16)],
    )(rows, mixed, results)


def solution(mesh):
    return jax.shard_map(
        shards,
        mesh=mesh,
        in_specs=(
            P(("seq", "grp"), None, None),
            P("seq", "grp", None),
            P(),
            P(),
            P(),
            P(),
            P(("seq", "grp"), None, None),
            P(("seq", "grp"), None, None),
            P(("seq", "grp"), None, None),
        ),
        out_specs=P(("seq", "grp"), None),
        check_vma=False,
    )
```

```python
import jax
import jax.numpy as jnp
from jax import lax
from jax.experimental import pallas as pl
from jax.experimental.pallas import tpu as pltpu
from jax.sharding import PartitionSpec as P

BF16 = jnp.bfloat16
F32 = jnp.float32
I32 = jnp.int32
ALL = ("seq", "grp")

SEQ = 8
GRP = 16
DEVICES = 128
ROWS = 128
HEAD = 128
WIDTH = 2048
CHUNKS = WIDTH // 128
CLUSTER = 1024
SLOTS = 12
LOW = 8
HIGH = 4
ESLOTS = 6
CHOSEN = 512
HIDDEN = 768
SENT = DEVICES * ESLOTS
GROUP = 32
FAR = -1e30
GROWS = GROUP * SLOTS
PLACES = DEVICES * SLOTS

NN = (((1,), (0,)), ((), ()))
NT = (((1,), (1,)), ((), ()))
TN = (((0,), (0,)), ((), ()))
VMEM_LIMIT = 60 * 1024 * 1024


def iota(shape, axis):
    return lax.broadcasted_iota(I32, shape, axis)


def dot(a, b, dims=NN):
    return lax.dot_general(a, b, dims, preferred_element_type=F32)


def whole(space=pltpu.VMEM):
    return pl.BlockSpec(memory_space=space)


def rank_in_block(block, most):
    lane = iota(block.shape, 1)
    rank = jnp.zeros(block.shape, I32)
    for back in range(1, most):
        same = (pltpu.roll(block, back, 1) == block) & (lane >= back)
        rank = rank + jnp.where(same, 1, 0)
    return rank


def request_kernel(lists_ref, out_ref):
    line = iota((128, CLUSTER), 0)
    asked = jnp.zeros((DEVICES, 128), F32)
    for h in range(2):
        token = lists_ref[h]
        block = token >> 7
        slot_line = h * 16 + rank_in_block(block, SLOTS)
        row = ((token & 127) + 1).astype(F32)
        member = jnp.where(block == line, 1.0, 0.0).astype(BF16)
        rows = jnp.where(slot_line == line, row, 0.0).astype(BF16)
        asked = asked + dot(member, rows, NT)
    out_ref[...] = asked


def place_order(index):
    group = index // GROWS
    inner = index - group * GROWS
    upper = inner - GROUP * LOW
    is_low = inner < GROUP * LOW
    source = group * GROUP + jnp.where(is_low, inner >> 3, upper >> 2)
    slot = jnp.where(is_low, inner & 7, LOW + (upper & 3))
    return source, slot


def empty_kernel(lists_ref, out_ref):
    line = iota((128, CLUSTER), 0)
    source, slot = place_order(iota((PLACES, 128), 0))
    lane = iota((PLACES, 128), 1)
    spread = jnp.where(lane == source, 1.0, 0.0).astype(BF16)
    for h in range(2):
        member = jnp.where((lists_ref[h] >> 7) == line, 1.0, 0.0).astype(BF16)
        count = dot(member, jnp.ones((CLUSTER, 128), BF16)).astype(BF16)
        held = dot(spread, count)
        empty = (slot.astype(F32) >= held) & (lane == 0)
        out_ref[h] = jnp.where(empty, FAR, 0.0).astype(BF16)


def expert_index_kernel(place_ref, lists_ref, marks_ref, rows_ref, slots_ref):
    me = place_ref[0]
    lists = lists_ref[...]
    inside = (lists >> 7) == me
    position = iota((DEVICES, CHOSEN), 1)
    before = jnp.sum(jnp.where(lists < me * ROWS, 1.0, 0.0), axis=1, keepdims=True).astype(I32)
    row = (lists - me * ROWS + 1).astype(F32)
    rank = jnp.where(inside, position - before, -1)
    lane = iota((DEVICES, 128), 1)
    rows = jnp.zeros((DEVICES, 128), F32)
    for k in range(ESLOTS):
        found = jnp.sum(jnp.where(rank == k, row, 0.0), axis=1, keepdims=True)
        rows = jnp.where(lane == k, found, rows)
    marks = rows.T[:8].astype(I32)
    marks_ref[...] = marks
    rows_ref[...] = jnp.maximum(marks - 1, 0)
    mine = lists_ref[pl.ds(me, 1), :]
    block = mine >> 7
    slots_ref[...] = block * ESLOTS + rank_in_block(block, ESLOTS)


def wanted_rows(asked):
    asked = asked.astype(BF16)
    line = iota((128, 128), 0)
    lane = iota((128, 128), 1)
    seq_of = jnp.where(iota((SEQ, 128), 1) >> 4 == iota((SEQ, 128), 0), 1.0, 0.0).astype(BF16)
    wanted = []
    for kind in range(3):
        slot = (lane & 7) + 16 * kind if kind < 2 else ((lane >> 2) & 1) * 16 + LOW + (lane & 3)
        placed = dot(asked, jnp.where(line == slot, 1.0, 0.0).astype(BF16))
        placed = jnp.where((line & 15) == lane >> 3, placed, 0.0).astype(BF16)
        wanted.append(dot(seq_of, placed))
    return wanted


def select_kernel(asked_ref, qkv_ref, wanted_ref, out_ref):
    wanted = wanted_rows(asked_ref[...])
    for kind in range(3):
        wanted_ref[kind] = wanted[kind]
    token = (iota((ROWS, 128), 0) + 1).astype(F32)
    lane_head = (iota((ROWS, 128), 1) >> 2) & 1
    for s in range(SEQ):
        peers = slice(s * GRP, (s + 1) * GRP)
        high_match = wanted[2][s : s + 1, :] == token
        high = jnp.zeros((128, 3 * HEAD), F32)
        for h in range(2):
            start = (2 * s + h) * HEAD
            packed = jnp.concatenate(
                [qkv_ref[c, :, start : start + HEAD] for c in range(3)], axis=1
            )
            low_match = jnp.where(wanted[h][s : s + 1, :] == token, 1.0, 0.0).astype(BF16)
            low = dot(low_match, packed, TN).astype(BF16)
            mine = jnp.where(high_match & (lane_head == h), 1.0, 0.0).astype(BF16)
            high = high + dot(mine, packed, TN)
            for c in range(3):
                out_ref[peers, h * 3 + c] = low[:, c * HEAD : (c + 1) * HEAD].reshape(GRP, 8, HEAD)
        high = high.astype(BF16)
        for c in range(3):
            out_ref[peers, 6 + c] = high[:, c * HEAD : (c + 1) * HEAD].reshape(GRP, 8, HEAD)


def attend_kernel(empty_ref, x_ref, out_ref, packed_ref, causal_ref):
    factor = HEAD ** (-0.5) * 1.4426950408889634
    low_rows = GROUP * LOW
    high_rows = GROUP * HIGH
    joint = iota((2 * high_rows, high_rows), 0)
    apart = iota((2 * high_rows, high_rows), 1)
    same_place = (joint >> 3) * HIGH + (joint & 3) == apart
    spread = [
        jnp.where(same_place & (((joint >> 2) & 1) == h), 1.0, 0.0).astype(BF16) for h in range(2)
    ]

    def order_of(index):
        source, slot = place_order(index)
        return source * SLOTS + slot

    later = order_of(iota((1, GROWS), 1)) > order_of(iota((GROWS, 1), 0))
    causal_ref[...] = jnp.where(later, FAR, 0.0)
    first_lane = jnp.where(iota((GROWS, 128), 1) == 0, 1.0, 0.0).astype(BF16)
    for i in range(DEVICES // GROUP):
        blocks = slice(i * GROUP, (i + 1) * GROUP)
        start, stop = i * GROWS, (i + 1) * GROWS
        for c in range(3):
            both = x_ref[blocks, 6 + c].reshape(2 * high_rows, HEAD)
            for h in range(2):
                packed_ref[h, c, start : start + low_rows, :] = x_ref[blocks, h * 3 + c].reshape(
                    low_rows, HEAD
                )
                packed_ref[h, c, start + low_rows : stop, :] = dot(spread[h], both, TN).astype(BF16)
        joined = jnp.zeros((2 * high_rows, HEAD), F32)
        for h in range(2):

            def keys(begin, end):
                return jnp.concatenate(
                    [packed_ref[h, 1, begin:end, :], empty_ref[h, begin:end, :]], axis=1
                )

            def values(begin, end):
                return jnp.concatenate(
                    [packed_ref[h, 2, begin:end, :], jnp.ones((end - begin, 128), BF16)], axis=1
                )

            queries = jnp.concatenate([packed_ref[h, 0, start:stop, :], first_lane], axis=1)
            near = dot(queries, keys(start, stop), NT) + causal_ref[...]
            top = jnp.max(near, axis=1, keepdims=True)
            if i:
                far = dot(queries, keys(0, start), NT)
                top = jnp.maximum(top, jnp.max(far, axis=1, keepdims=True))
            near = jnp.exp2((near - top) * factor).astype(BF16)
            summed = dot(near, values(start, stop))
            if i:
                far = jnp.exp2((far - top) * factor).astype(BF16)
                summed = summed + dot(far, values(0, start))
            result = (summed[:, :HEAD] / summed[:, HEAD:]).astype(BF16)
            out_ref[blocks, h] = result[:low_rows].reshape(GROUP, 8, HEAD)
            joined = joined + dot(spread[h], result[low_rows:])
        out_ref[blocks, 2] = joined.astype(BF16).reshape(GROUP, 8, HEAD)


def mix_kernel(
    rows_ref, wanted_ref, came_ref, w_out_ref, gain_ref, mixed_ref, out_hbm,
    w_ref, att_ref, tall_ref, tile_ref, out_ref, w_sems, out_sems,
):
    parts = w_sems.shape[0]
    depth = WIDTH // parts
    copies = [
        pltpu.make_async_copy(
            w_out_ref.at[pl.ds(p * depth, depth), :], w_ref.at[pl.ds(p * depth, depth), :], w_sems.at[p]
        )
        for p in range(parts)
    ]
    for copy in copies:
        copy.start()
    token = (iota((ROWS, 128), 0) + 1).astype(F32)
    lane_head = (iota((ROWS, 128), 1) >> 2) & 1
    for s in range(SEQ):
        peers = slice(s * GRP, (s + 1) * GRP)
        high_match = wanted_ref[2, s : s + 1, :] == token
        high = came_ref[peers, 2].reshape(128, HEAD)
        for h in range(2):
            low_match = jnp.where(wanted_ref[h, s : s + 1, :] == token, 1.0, 0.0).astype(BF16)
            mine = jnp.where(high_match & (lane_head == h), 1.0, 0.0).astype(BF16)
            got = dot(
                jnp.concatenate([low_match, mine], axis=1),
                jnp.concatenate([came_ref[peers, h].reshape(128, HEAD), high], axis=0),
            )
            start = (2 * s + h) * HEAD
            att_ref[:, start : start + HEAD] = got.astype(BF16)
    total = jnp.zeros((ROWS, WIDTH), F32)
    for p in range(parts):
        copies[p].wait()
        total = total + dot(
            att_ref[:, p * depth : (p + 1) * depth], w_ref[p * depth : (p + 1) * depth, :]
        )
    mixed = total.astype(BF16)
    mixed_ref[...] = mixed
    wide = mixed.astype(F32)
    mean_square = jnp.mean(wide * wide, axis=1, keepdims=True)
    normed = wide * lax.rsqrt(mean_square + 1e-06) * gain_ref[...].astype(F32)
    for j in range(CHUNKS):
        tall_ref[pl.ds(j, ROWS, stride=CHUNKS), :] = normed[:, j * 128 : (j + 1) * 128]
    tile_ref[...] = tall_ref[...].astype(BF16).reshape(ROWS, CHUNKS, 128)
    sends = out_sems.shape[0]
    share = DEVICES // sends
    outs = []
    for p in range(sends):
        for e in range(p * share, (p + 1) * share):
            for k in range(ESLOTS):
                out_ref[e * ESLOTS + k] = tile_ref[rows_ref[k, e]]
        span = pl.ds(p * share * ESLOTS, share * ESLOTS)
        outs.append(pltpu.make_async_copy(out_ref.at[span], out_hbm.at[span], out_sems.at[p]))
        outs[-1].start()
    for copy in outs:
        copy.wait()


def expert_kernel(
    place_ref, slots_ref, x_ref, gate_hbm, up_hbm, down_hbm, router_ref, out_ref,
    gate_ref, up_ref, down_ref, tall_ref, rows_ref, hidden_ref, back_ref, sems,
):
    copies = [
        pltpu.make_async_copy(source.at[0], target, sems.at[n])
        for n, (source, target) in enumerate(
            [(gate_hbm, gate_ref), (up_hbm, up_ref), (down_hbm, down_ref)]
        )
    ]
    for copy in copies:
        copy.start()
    parts, half = rows_ref.shape[:2]
    me = place_ref[0]

    def take(part, begin, end):
        for i in range(begin, end):
            tall_ref[part, i * CHUNKS : (i + 1) * CHUNKS, :] = x_ref[
                slots_ref[0, part * half + i]
            ].astype(F32)

    def flatten(part, begin, end):
        for j in range(begin, end):
            rows_ref[part, :, j * 128 : (j + 1) * 128] = tall_ref[
                part, pl.ds(j, half, stride=CHUNKS), :
            ].astype(BF16)

    def put(part, begin, end):
        for i in range(begin, end):
            out_ref[slots_ref[0, part * half + i]] = back_ref[
                part, i * CHUNKS : (i + 1) * CHUNKS, :
            ].astype(BF16)

    take(0, 0, half)
    flatten(0, 0, CHUNKS)
    wide = HIDDEN // 3
    for part in range(parts):
        for n in range(3):
            columns = slice(n * wide, (n + 1) * wide)
            if part == 0 and n == 0:
                copies[0].wait()
            gate = dot(rows_ref[part], gate_ref[:, columns])
            if part == 0 and n == 0:
                copies[1].wait()
            up = dot(rows_ref[part], up_ref[:, columns])
            if part == 0:
                if n < 2:
                    out_ref[n * SENT // 2 : (n + 1) * SENT // 2] = jnp.zeros(
                        (SENT // 2, CHUNKS, 128), BF16
                    )
                    take(1, n * half // 2, (n + 1) * half // 2)
                else:
                    flatten(1, 0, CHUNKS)
            else:
                put(0, n * half // 3, (n + 1) * half // 3)
            hidden_ref[part, :, columns] = (jax.nn.silu(gate) * up).astype(BF16)
        logits = dot(rows_ref[part], router_ref[...])
        mine = jnp.where(iota((half, 128), 1) == me, logits, 0.0)
        weight = jax.nn.sigmoid(jnp.sum(mine, axis=1, keepdims=True))
        if part == 0:
            copies[2].wait()
        for n in range(4):
            result = dot(hidden_ref[part], down_ref[:, n * 512 : (n + 1) * 512]) * weight
            for j in range(4):
                back_ref[part, pl.ds(4 * n + j, half, stride=CHUNKS), :] = result[
                    :, j * 128 : (j + 1) * 128
                ]
    put(1, 0, half)


def combine_kernel(marks_ref, mixed_ref, x_ref, out_ref, tall_ref):
    for e in range(DEVICES):
        for k in range(ESLOTS):
            start = (k * DEVICES + e) * CHUNKS
            tall_ref[start : start + CHUNKS, :] = x_ref[e * ESLOTS + k].astype(F32)
    token = iota((ROWS, DEVICES), 0) + 1
    match = jnp.concatenate(
        [jnp.where(marks_ref[k : k + 1, :] == token, 1.0, 0.0) for k in range(ESLOTS)], axis=1
    ).astype(BF16)
    for n in range(CHUNKS // 2):
        flat = jnp.concatenate(
            [
                tall_ref[pl.ds(2 * n + j, SENT, stride=CHUNKS), :].astype(BF16)
                for j in range(2)
            ],
            axis=1,
        )
        columns = slice(n * 256, (n + 1) * 256)
        out_ref[:, columns] = (mixed_ref[:, columns].astype(F32) + dot(match, flat)).astype(BF16)


def call(kernel, out_shape, in_specs, scratch=(), out_specs=None):
    return pl.pallas_call(
        kernel,
        out_shape=out_shape,
        in_specs=in_specs,
        out_specs=jax.tree.map(lambda _: whole(), out_shape) if out_specs is None else out_specs,
        scratch_shapes=list(scratch),
        compiler_params=pltpu.CompilerParams(vmem_limit_bytes=VMEM_LIMIT),
    )


def shape(dims, dtype=BF16):
    return jax.ShapeDtypeStruct(dims, dtype)


def exchange(array):
    return lax.all_to_all(array, ALL, split_axis=0, concat_axis=0, tiled=True)


def near(array):
    return pltpu.with_memory_space_constraint(array, pltpu.VMEM)


def shards(qkv, cluster_lists, w_out, norm_gain, router, expert_lists, w_gate, w_up, w_down):
    me = lax.axis_index("seq") * GRP + lax.axis_index("grp")
    place = me.reshape(1).astype(I32)
    smem = whole(pltpu.SMEM)
    hbm = whole(pl.ANY)

    request = call(request_kernel, shape((DEVICES, 128), F32), [whole()])(cluster_lists)
    asked = exchange(request.reshape(DEVICES, 1, 128)).reshape(DEVICES, 128)
    empty = call(empty_kernel, shape((2, PLACES, 128)), [whole()])(cluster_lists)
    marks, rows, slots = call(
        expert_index_kernel,
        (shape((8, DEVICES), I32), shape((8, DEVICES), I32), shape((1, CHOSEN), I32)),
        [smem, whole()],
    )(place, expert_lists)

    wanted, picked = call(
        select_kernel,
        (shape((3, SEQ, 128), F32), shape((DEVICES, 9, 8, HEAD))),
        [whole(), whole()],
    )(asked, near(qkv.transpose(1, 0, 2)))
    arrived = exchange(picked)

    outputs = call(
        attend_kernel,
        shape((DEVICES, 3, 8, HEAD)),
        [whole(), whole()],
        [pltpu.VMEM((2, 3, PLACES, HEAD), BF16), pltpu.VMEM((GROWS, GROWS), F32)],
    )(empty, near(arrived))
    came_back = exchange(outputs)

    mixed, outgoing = call(
        mix_kernel,
        (shape((ROWS, WIDTH)), shape((SENT, CHUNKS, 128))),
        [smem, whole(), whole(), hbm, whole()],
        [
            pltpu.VMEM((WIDTH, WIDTH), BF16),
            pltpu.VMEM((ROWS, WIDTH), BF16),
            pltpu.VMEM((ROWS * CHUNKS, 128), F32),
            pltpu.VMEM((ROWS, CHUNKS, 128), BF16),
            pltpu.VMEM((SENT, CHUNKS, 128), BF16),
            pltpu.SemaphoreType.DMA((4,)),
            pltpu.SemaphoreType.DMA((4,)),
        ],
        out_specs=(whole(), hbm),
    )(rows, wanted, near(came_back), w_out, norm_gain.reshape(1, WIDTH))
    incoming = exchange(outgoing)

    half = CHOSEN // 2
    produced = call(
        expert_kernel,
        shape((SENT, CHUNKS, 128)),
        [smem, smem, whole(), hbm, hbm, hbm, whole()],
        [
            pltpu.VMEM((WIDTH, HIDDEN), BF16),
            pltpu.VMEM((WIDTH, HIDDEN), BF16),
            pltpu.VMEM((HIDDEN, WIDTH), BF16),
            pltpu.VMEM((2, half * CHUNKS, 128), F32),
            pltpu.VMEM((2, half, WIDTH), BF16),
            pltpu.VMEM((2, half, HIDDEN), BF16),
            pltpu.VMEM((2, half * CHUNKS, 128), F32),
            pltpu.SemaphoreType.DMA((3,)),
        ],
    )(place, slots, incoming, w_gate, w_up, w_down, router)
    results = exchange(produced)

    return call(
        combine_kernel,
        shape((ROWS, WIDTH)),
        [whole(), whole(), whole()],
        [pltpu.VMEM((SENT * CHUNKS, 128), F32)],
    )(marks, mixed, results)


def solution(mesh):
    return jax.shard_map(
        shards,
        mesh=mesh,
        in_specs=(
            P(("seq", "grp"), None, None),
            P("seq", "grp", None),
            P(),
            P(),
            P(),
            P(),
            P(("seq", "grp"), None, None),
            P(("seq", "grp"), None, None),
            P(("seq", "grp"), None, None),
        ),
        out_specs=P(("seq", "grp"), None),
        check_vma=False,
    )
```

```python
import jax
import jax.numpy as jnp
from jax import lax
from jax.experimental import pallas as pl
from jax.experimental.pallas import tpu as pltpu
from jax.sharding import PartitionSpec as P

BF16 = jnp.bfloat16
F32 = jnp.float32
I32 = jnp.int32
ALL = ("seq", "grp")

SEQ = 8
GRP = 16
DEVICES = 128
ROWS = 128
HEAD = 128
WIDTH = 2048
CHUNKS = WIDTH // 128
CLUSTER = 1024
SLOTS = 12
LOW = 8
HIGH = 4
ESLOTS = 6
CHOSEN = 512
HIDDEN = 768
SENT = DEVICES * ESLOTS
GROUP = 32
FAR = -1e30
PIECES = 3
PITCH = CHUNKS + 1
GROWS = GROUP * SLOTS
PLACES = DEVICES * SLOTS

NN = (((1,), (0,)), ((), ()))
NT = (((1,), (1,)), ((), ()))
TN = (((0,), (0,)), ((), ()))
VMEM_LIMIT = 60 * 1024 * 1024


def iota(shape, axis):
    return lax.broadcasted_iota(I32, shape, axis)


def dot(a, b, dims=NN):
    return lax.dot_general(a, b, dims, preferred_element_type=F32)


def whole(space=pltpu.VMEM):
    return pl.BlockSpec(memory_space=space)


def rank_in_block(block, most):
    lane = iota(block.shape, 1)
    rank = jnp.zeros(block.shape, I32)
    for back in range(1, most):
        same = (pltpu.roll(block, back, 1) == block) & (lane >= back)
        rank = rank + jnp.where(same, 1, 0)
    return rank


def request_kernel(lists_ref, out_ref):
    line = iota((128, CLUSTER), 0)
    asked = jnp.zeros((DEVICES, 128), F32)
    for h in range(2):
        token = lists_ref[h]
        block = token >> 7
        slot_line = h * 16 + rank_in_block(block, SLOTS)
        row = ((token & 127) + 1).astype(F32)
        member = jnp.where(block == line, 1.0, 0.0).astype(BF16)
        rows = jnp.where(slot_line == line, row, 0.0).astype(BF16)
        asked = asked + dot(member, rows, NT)
    out_ref[...] = asked


def place_order(index):
    group = index // GROWS
    inner = index - group * GROWS
    upper = inner - GROUP * LOW
    is_low = inner < GROUP * LOW
    source = group * GROUP + jnp.where(is_low, inner >> 3, upper >> 2)
    slot = jnp.where(is_low, inner & 7, LOW + (upper & 3))
    return source, slot


def empty_kernel(lists_ref, out_ref):
    line = iota((128, CLUSTER), 0)
    source, slot = place_order(iota((1, PLACES), 1))
    spread = jnp.where(iota((128, PLACES), 0) == source, 1.0, 0.0).astype(BF16)
    for h in range(2):
        member = jnp.where((lists_ref[h] >> 7) == line, 1.0, 0.0).astype(BF16)
        count = dot(jnp.ones((8, CLUSTER), BF16), member, NT)
        held = dot(count.astype(BF16), spread)
        out_ref[h] = jnp.where(slot.astype(F32) < held, 0.0, FAR)


def expert_index_kernel(place_ref, lists_ref, marks_ref, rows_ref, slots_ref):
    me = place_ref[0]
    lists = lists_ref[...]
    inside = (lists >> 7) == me
    position = iota((DEVICES, CHOSEN), 1)
    before = jnp.sum(jnp.where(lists < me * ROWS, 1.0, 0.0), axis=1, keepdims=True).astype(I32)
    row = (lists - me * ROWS + 1).astype(F32)
    rank = jnp.where(inside, position - before, -1)
    lane = iota((DEVICES, 128), 1)
    rows = jnp.zeros((DEVICES, 128), F32)
    for k in range(ESLOTS):
        found = jnp.sum(jnp.where(rank == k, row, 0.0), axis=1, keepdims=True)
        rows = jnp.where(lane == k, found, rows)
    marks = rows.T[:8].astype(I32)
    marks_ref[...] = marks
    rows_ref[...] = jnp.maximum(marks - 1, 0)
    mine = lists_ref[pl.ds(me, 1), :]
    block = mine >> 7
    slots_ref[...] = block * ESLOTS + rank_in_block(block, ESLOTS)


def wanted_rows(asked):
    asked = asked.astype(BF16)
    line = iota((128, 128), 0)
    lane = iota((128, 128), 1)
    seq_of = jnp.where(iota((SEQ, 128), 1) >> 4 == iota((SEQ, 128), 0), 1.0, 0.0).astype(BF16)
    wanted = []
    for kind in range(3):
        slot = (lane & 7) + 16 * kind if kind < 2 else ((lane >> 2) & 1) * 16 + LOW + (lane & 3)
        placed = dot(asked, jnp.where(line == slot, 1.0, 0.0).astype(BF16))
        placed = jnp.where((line & 15) == lane >> 3, placed, 0.0).astype(BF16)
        wanted.append(dot(seq_of, placed))
    return wanted


def select_kernel(asked_ref, qkv_ref, wanted_ref, out_ref):
    wanted = wanted_rows(asked_ref[...])
    for kind in range(3):
        wanted_ref[kind] = wanted[kind]
    token = (iota((ROWS, 128), 0) + 1).astype(F32)
    lane_head = (iota((ROWS, 128), 1) >> 2) & 1
    for s in range(SEQ):
        peers = slice(s * GRP, (s + 1) * GRP)
        high_match = wanted[2][s : s + 1, :] == token
        high = jnp.zeros((128, 3 * HEAD), F32)
        for h in range(2):
            start = (2 * s + h) * HEAD
            packed = jnp.concatenate(
                [qkv_ref[c, :, start : start + HEAD] for c in range(3)], axis=1
            )
            low_match = jnp.where(wanted[h][s : s + 1, :] == token, 1.0, 0.0).astype(BF16)
            low = dot(low_match, packed, TN).astype(BF16)
            mine = jnp.where(high_match & (lane_head == h), 1.0, 0.0).astype(BF16)
            high = high + dot(mine, packed, TN)
            for c in range(3):
                out_ref[peers, h * 3 + c] = low[:, c * HEAD : (c + 1) * HEAD].reshape(GRP, 8, HEAD)
        high = high.astype(BF16)
        for c in range(3):
            out_ref[peers, 6 + c] = high[:, c * HEAD : (c + 1) * HEAD].reshape(GRP, 8, HEAD)


def attend_kernel(empty_ref, x_ref, out_ref, packed_ref, causal_ref, result_ref):
    factor = HEAD ** (-0.5) * 1.4426950408889634
    low_rows = GROUP * LOW
    high_rows = GROUP * HIGH
    joint = iota((2 * high_rows, high_rows), 0)
    apart = iota((2 * high_rows, high_rows), 1)
    same_place = (joint >> 3) * HIGH + (joint & 3) == apart
    spread = [
        jnp.where(same_place & (((joint >> 2) & 1) == h), 1.0, 0.0).astype(BF16) for h in range(2)
    ]

    def order_of(index):
        source, slot = place_order(index)
        return source * SLOTS + slot

    later = order_of(iota((1, GROWS), 1)) > order_of(iota((GROWS, 1), 0))
    causal_ref[...] = jnp.where(later, FAR, 0.0)
    groups = DEVICES // GROUP
    for i in range(groups):
        blocks = slice(i * GROUP, (i + 1) * GROUP)
        start, stop = i * GROWS, (i + 1) * GROWS
        for c in range(3):
            both = x_ref[blocks, 6 + c].reshape(2 * high_rows, HEAD)
            for h in range(2):
                packed_ref[h, c, start : start + low_rows, :] = x_ref[blocks, h * 3 + c].reshape(
                    low_rows, HEAD
                )
                packed_ref[h, c, start + low_rows : stop, :] = dot(spread[h], both, TN).astype(BF16)

    piece = GROWS // PIECES

    def score(i, h, q):
        start, stop = i * GROWS, (i + 1) * GROWS
        inner = slice(q * piece, (q + 1) * piece)
        queries = packed_ref[h, 0, start + q * piece : start + (q + 1) * piece, :]
        near = dot(queries, packed_ref[h, 1, start:stop, :], NT)
        near = near + causal_ref[inner, :] + empty_ref[h, 0:1, start:stop]
        if i == 0:
            return (near,)
        far = dot(queries, packed_ref[h, 1, :start, :], NT) + empty_ref[h, 0:1, :start]
        return (near, far)

    def finish(i, h, q, scores):
        start, stop = i * GROWS, (i + 1) * GROWS
        top = jnp.max(scores[0], axis=1, keepdims=True)
        for part in scores[1:]:
            top = jnp.maximum(top, jnp.max(part, axis=1, keepdims=True))
        summed = jnp.zeros((piece, 2 * HEAD), F32)
        for part, (begin, end) in zip(scores, ((start, stop), (0, start))):
            weights = jnp.exp2((part - top) * factor).astype(BF16)
            values = jnp.concatenate(
                [packed_ref[h, 2, begin:end, :], jnp.ones((end - begin, 128), BF16)], axis=1
            )
            summed = summed + dot(weights, values)
        result_ref[q * piece : (q + 1) * piece, :] = (summed[:, :HEAD] / summed[:, HEAD:]).astype(BF16)

    steps = [(i, h, q) for i in range(groups) for h in range(2) for q in range(PIECES)]
    ready = score(*steps[0])
    joined = None
    for n, (i, h, q) in enumerate(steps):
        scores = ready
        if n + 1 < len(steps):
            ready = score(*steps[n + 1])
        finish(i, h, q, scores)
        if q < PIECES - 1:
            continue
        blocks = slice(i * GROUP, (i + 1) * GROUP)
        out_ref[blocks, h] = result_ref[:low_rows].reshape(GROUP, 8, HEAD)
        part = dot(spread[h], result_ref[low_rows:])
        joined = part if h == 0 else joined + part
        if h == 1:
            out_ref[blocks, 2] = joined.astype(BF16).reshape(GROUP, 8, HEAD)


def mix_kernel(
    rows_ref, wanted_ref, came_ref, w_out_ref, gain_ref, mixed_ref, out_hbm,
    w_ref, att_ref, tall_ref, tile_ref, out_ref, w_sems, out_sems,
):
    parts = w_sems.shape[0]
    span = WIDTH // parts
    copies = [
        pltpu.make_async_copy(w_out_ref.at[:, pl.ds(p * span, span)], w_ref.at[p], w_sems.at[p])
        for p in range(parts)
    ]
    for copy in copies:
        copy.start()
    token = (iota((ROWS, 128), 0) + 1).astype(F32)
    lane_head = (iota((ROWS, 128), 1) >> 2) & 1
    for s in range(SEQ):
        peers = slice(s * GRP, (s + 1) * GRP)
        high_match = wanted_ref[2, s : s + 1, :] == token
        high = came_ref[peers, 2].reshape(128, HEAD)
        for h in range(2):
            low_match = jnp.where(wanted_ref[h, s : s + 1, :] == token, 1.0, 0.0).astype(BF16)
            mine = jnp.where(high_match & (lane_head == h), 1.0, 0.0).astype(BF16)
            got = dot(
                jnp.concatenate([low_match, mine], axis=1),
                jnp.concatenate([came_ref[peers, h].reshape(128, HEAD), high], axis=0),
            )
            start = (2 * s + h) * HEAD
            att_ref[:, start : start + HEAD] = got.astype(BF16)
    attended = att_ref[...]
    for p in range(parts):
        copies[p].wait()
        mixed_ref[:, p * span : (p + 1) * span] = dot(attended, w_ref[p]).astype(BF16)
    wide = mixed_ref[...].astype(F32)
    mean_square = jnp.mean(wide * wide, axis=1, keepdims=True)
    normed = wide * lax.rsqrt(mean_square + 1e-06) * gain_ref[...].astype(F32)
    for j in range(CHUNKS):
        tall_ref[pl.ds(j, ROWS, stride=PITCH), :] = normed[:, j * 128 : (j + 1) * 128]
    for t in range(ROWS):
        tile_ref[t] = tall_ref[t * PITCH : t * PITCH + CHUNKS, :].astype(BF16)
    sends = out_sems.shape[0]
    share = DEVICES // sends
    outs = []
    for p in range(sends):
        for e in range(p * share, (p + 1) * share):
            for k in range(ESLOTS):
                out_ref[e * ESLOTS + k] = tile_ref[rows_ref[k, e]]
        span = pl.ds(p * share * ESLOTS, share * ESLOTS)
        outs.append(pltpu.make_async_copy(out_ref.at[span], out_hbm.at[span], out_sems.at[p]))
        outs[-1].start()
    for copy in outs:
        copy.wait()


def expert_kernel(
    place_ref, slots_ref, x_hbm, gate_hbm, up_hbm, down_hbm, router_ref, out_ref,
    x_ref, gate_ref, up_ref, down_ref, tall_ref, rows_ref, hidden_ref, sems,
):
    arrival = pltpu.make_async_copy(x_hbm, x_ref, sems.at[3])
    arrival.start()
    copies = [
        pltpu.make_async_copy(source.at[0], target, sems.at[n])
        for n, (source, target) in enumerate(
            [(gate_hbm, gate_ref), (up_hbm, up_ref), (down_hbm, down_ref)]
        )
    ]
    for copy in copies:
        copy.start()
    out_ref[...] = jnp.zeros(out_ref.shape, BF16)
    arrival.wait()
    me = place_ref[0]
    for i in range(CHOSEN):
        tall_ref[i * PITCH : i * PITCH + CHUNKS, :] = x_ref[slots_ref[0, i]].astype(F32)
    for j in range(CHUNKS):
        rows_ref[:, j * 128 : (j + 1) * 128] = tall_ref[pl.ds(j, CHOSEN, stride=PITCH), :].astype(BF16)
    rows = rows_ref[...]
    wide = HIDDEN // 3
    for n in range(3):
        columns = slice(n * wide, (n + 1) * wide)
        if n == 0:
            copies[0].wait()
        gate = dot(rows, gate_ref[:, columns])
        if n == 0:
            copies[1].wait()
        up = dot(rows, up_ref[:, columns])
        hidden_ref[:, columns] = (jax.nn.silu(gate) * up).astype(BF16)
    logits = dot(rows, router_ref[...])
    mine = jnp.where(iota((CHOSEN, 128), 1) == me, logits, 0.0)
    weight = jax.nn.sigmoid(jnp.sum(mine, axis=1, keepdims=True))
    copies[2].wait()
    hidden = hidden_ref[...]
    for n in range(8):
        result = dot(hidden, down_ref[:, n * 256 : (n + 1) * 256]) * weight
        for j in range(2):
            tall_ref[pl.ds(2 * n + j, CHOSEN, stride=PITCH), :] = result[:, j * 128 : (j + 1) * 128]
    for i in range(CHOSEN):
        out_ref[slots_ref[0, i]] = tall_ref[i * PITCH : i * PITCH + CHUNKS, :].astype(BF16)


def combine_kernel(marks_ref, mixed_ref, x_ref, out_ref, tall_ref):
    for e in range(DEVICES):
        for k in range(ESLOTS):
            start = (k * DEVICES + e) * PITCH
            tall_ref[start : start + CHUNKS, :] = x_ref[e * ESLOTS + k].astype(F32)
    token = iota((ROWS, DEVICES), 0) + 1
    match = jnp.concatenate(
        [jnp.where(marks_ref[k : k + 1, :] == token, 1.0, 0.0) for k in range(ESLOTS)], axis=1
    ).astype(BF16)
    for n in range(CHUNKS // 2):
        flat = jnp.concatenate(
            [
                tall_ref[pl.ds(2 * n + j, SENT, stride=PITCH), :].astype(BF16)
                for j in range(2)
            ],
            axis=1,
        )
        columns = slice(n * 256, (n + 1) * 256)
        out_ref[:, columns] = (mixed_ref[:, columns].astype(F32) + dot(match, flat)).astype(BF16)


def call(kernel, out_shape, in_specs, scratch=(), out_specs=None):
    return pl.pallas_call(
        kernel,
        out_shape=out_shape,
        in_specs=in_specs,
        out_specs=jax.tree.map(lambda _: whole(), out_shape) if out_specs is None else out_specs,
        scratch_shapes=list(scratch),
        compiler_params=pltpu.CompilerParams(vmem_limit_bytes=VMEM_LIMIT),
    )


def shape(dims, dtype=BF16):
    return jax.ShapeDtypeStruct(dims, dtype)


def exchange(array):
    return lax.all_to_all(array, ALL, split_axis=0, concat_axis=0, tiled=True)


def near(array):
    return pltpu.with_memory_space_constraint(array, pltpu.VMEM)


def shards(qkv, cluster_lists, w_out, norm_gain, router, expert_lists, w_gate, w_up, w_down):
    me = lax.axis_index("seq") * GRP + lax.axis_index("grp")
    place = me.reshape(1).astype(I32)
    smem = whole(pltpu.SMEM)
    hbm = whole(pl.ANY)

    request = call(request_kernel, shape((DEVICES, 128), F32), [whole()])(cluster_lists)
    asked = exchange(request.reshape(DEVICES, 1, 128)).reshape(DEVICES, 128)
    empty = call(empty_kernel, shape((2, 8, PLACES), F32), [whole()])(cluster_lists)
    marks, rows, slots = call(
        expert_index_kernel,
        (shape((8, DEVICES), I32), shape((8, DEVICES), I32), shape((1, CHOSEN), I32)),
        [smem, whole()],
    )(place, expert_lists)

    wanted, picked = call(
        select_kernel,
        (shape((3, SEQ, 128), F32), shape((DEVICES, 9, 8, HEAD))),
        [whole(), whole()],
    )(asked, qkv.transpose(1, 0, 2))
    arrived = exchange(picked)

    outputs = call(
        attend_kernel,
        shape((DEVICES, 3, 8, HEAD)),
        [whole(), whole()],
        [
            pltpu.VMEM((2, 3, PLACES, HEAD), BF16),
            pltpu.VMEM((GROWS, GROWS), F32),
            pltpu.VMEM((GROWS, HEAD), BF16),
        ],
    )(empty, near(arrived))
    came_back = exchange(outputs)

    mixed, outgoing = call(
        mix_kernel,
        (shape((ROWS, WIDTH)), shape((SENT, CHUNKS, 128))),
        [smem, whole(), whole(), hbm, whole()],
        [
            pltpu.VMEM((4, WIDTH, WIDTH // 4), BF16),
            pltpu.VMEM((ROWS, WIDTH), BF16),
            pltpu.VMEM((ROWS * PITCH, 128), F32),
            pltpu.VMEM((ROWS, CHUNKS, 128), BF16),
            pltpu.VMEM((SENT, CHUNKS, 128), BF16),
            pltpu.SemaphoreType.DMA((4,)),
            pltpu.SemaphoreType.DMA((4,)),
        ],
        out_specs=(whole(), hbm),
    )(rows, wanted, near(came_back), w_out, norm_gain.reshape(1, WIDTH))
    incoming = exchange(outgoing)

    produced = call(
        expert_kernel,
        shape((SENT, CHUNKS, 128)),
        [smem, smem, hbm, hbm, hbm, hbm, whole()],
        [
            pltpu.VMEM((SENT, CHUNKS, 128), BF16),
            pltpu.VMEM((WIDTH, HIDDEN), BF16),
            pltpu.VMEM((WIDTH, HIDDEN), BF16),
            pltpu.VMEM((HIDDEN, WIDTH), BF16),
            pltpu.VMEM((CHOSEN * PITCH, 128), F32),
            pltpu.VMEM((CHOSEN, WIDTH), BF16),
            pltpu.VMEM((CHOSEN, HIDDEN), BF16),
            pltpu.SemaphoreType.DMA((4,)),
        ],
    )(place, slots, incoming, w_gate, w_up, w_down, router)
    results = exchange(produced)

    return call(
        combine_kernel,
        shape((ROWS, WIDTH)),
        [whole(), whole(), whole()],
        [pltpu.VMEM((SENT * PITCH, 128), F32)],
    )(marks, mixed, results)


def solution(mesh):
    return jax.shard_map(
        shards,
        mesh=mesh,
        in_specs=(
            P(("seq", "grp"), None, None),
            P("seq", "grp", None),
            P(),
            P(),
            P(),
            P(),
            P(("seq", "grp"), None, None),
            P(("seq", "grp"), None, None),
            P(("seq", "grp"), None, None),
        ),
        out_specs=P(("seq", "grp"), None),
        check_vma=False,
    )
```

```python
import jax
import jax.numpy as jnp
from jax import lax
from jax.experimental import pallas as pl
from jax.experimental.pallas import tpu as pltpu
from jax.sharding import PartitionSpec as P

BF16 = jnp.bfloat16
F32 = jnp.float32
I32 = jnp.int32
ALL = ("seq", "grp")

SEQ = 8
GRP = 16
DEVICES = 128
ROWS = 128
HEAD = 128
WIDTH = 2048
CHUNKS = WIDTH // 128
CLUSTER = 1024
SLOTS = 12
LOW = 8
HIGH = 4
ESLOTS = 6
CHOSEN = 512
HIDDEN = 768
SENT = DEVICES * ESLOTS
GROUP = 32
FAR = -1e30
PIECES = 3
PITCH = CHUNKS + 1
GROWS = GROUP * SLOTS
PLACES = DEVICES * SLOTS

NN = (((1,), (0,)), ((), ()))
NT = (((1,), (1,)), ((), ()))
TN = (((0,), (0,)), ((), ()))
VMEM_LIMIT = 60 * 1024 * 1024


def iota(shape, axis):
    return lax.broadcasted_iota(I32, shape, axis)


def dot(a, b, dims=NN):
    return lax.dot_general(a, b, dims, preferred_element_type=F32)


def whole(space=pltpu.VMEM):
    return pl.BlockSpec(memory_space=space)


def rank_in_block(block, most):
    lane = iota(block.shape, 1)
    rank = jnp.zeros(block.shape, I32)
    for back in range(1, most):
        same = (pltpu.roll(block, back, 1) == block) & (lane >= back)
        rank = rank + jnp.where(same, 1, 0)
    return rank


def request_kernel(lists_ref, out_ref):
    line = iota((128, CLUSTER), 0)
    asked = jnp.zeros((DEVICES, 128), F32)
    for h in range(2):
        token = lists_ref[h]
        block = token >> 7
        slot_line = h * 16 + rank_in_block(block, SLOTS)
        row = ((token & 127) + 1).astype(F32)
        member = jnp.where(block == line, 1.0, 0.0).astype(BF16)
        rows = jnp.where(slot_line == line, row, 0.0).astype(BF16)
        asked = asked + dot(member, rows, NT)
    out_ref[...] = asked


def place_order(index):
    group = index // GROWS
    inner = index - group * GROWS
    upper = inner - GROUP * LOW
    is_low = inner < GROUP * LOW
    source = group * GROUP + jnp.where(is_low, inner >> 3, upper >> 2)
    slot = jnp.where(is_low, inner & 7, LOW + (upper & 3))
    return source, slot


def empty_kernel(lists_ref, out_ref):
    line = iota((128, CLUSTER), 0)
    source, slot = place_order(iota((1, PLACES), 1))
    spread = jnp.where(iota((128, PLACES), 0) == source, 1.0, 0.0).astype(BF16)
    for h in range(2):
        member = jnp.where((lists_ref[h] >> 7) == line, 1.0, 0.0).astype(BF16)
        count = dot(jnp.ones((8, CLUSTER), BF16), member, NT)
        held = dot(count.astype(BF16), spread)
        out_ref[h] = jnp.where(slot.astype(F32) < held, 0.0, FAR)


def expert_index_kernel(place_ref, lists_ref, marks_ref, rows_ref, slots_ref):
    me = place_ref[0]
    lists = lists_ref[...]
    inside = (lists >> 7) == me
    position = iota((DEVICES, CHOSEN), 1)
    before = jnp.sum(jnp.where(lists < me * ROWS, 1.0, 0.0), axis=1, keepdims=True).astype(I32)
    row = (lists - me * ROWS + 1).astype(F32)
    rank = jnp.where(inside, position - before, -1)
    lane = iota((DEVICES, 128), 1)
    rows = jnp.zeros((DEVICES, 128), F32)
    for k in range(ESLOTS):
        found = jnp.sum(jnp.where(rank == k, row, 0.0), axis=1, keepdims=True)
        rows = jnp.where(lane == k, found, rows)
    marks = rows.T[:8].astype(I32)
    marks_ref[...] = marks
    rows_ref[...] = jnp.maximum(marks - 1, 0)
    mine = lists_ref[pl.ds(me, 1), :]
    block = mine >> 7
    slots_ref[...] = block * ESLOTS + rank_in_block(block, ESLOTS)


def wanted_rows(asked):
    asked = asked.astype(BF16)
    line = iota((128, 128), 0)
    lane = iota((128, 128), 1)
    seq_of = jnp.where(iota((SEQ, 128), 1) >> 4 == iota((SEQ, 128), 0), 1.0, 0.0).astype(BF16)
    wanted = []
    for kind in range(3):
        slot = (lane & 7) + 16 * kind if kind < 2 else ((lane >> 2) & 1) * 16 + LOW + (lane & 3)
        placed = dot(asked, jnp.where(line == slot, 1.0, 0.0).astype(BF16))
        placed = jnp.where((line & 15) == lane >> 3, placed, 0.0).astype(BF16)
        wanted.append(dot(seq_of, placed))
    return wanted


def select_kernel(asked_ref, qkv_hbm, wanted_ref, out_hbm, qkv_ref, out_ref, in_sems, out_sems):
    parts = in_sems.shape[0]
    share = SEQ // parts
    width = WIDTH // parts
    copies = [
        pltpu.make_async_copy(
            qkv_hbm.at[:, :, pl.ds(p * width, width)], qkv_ref.at[p], in_sems.at[p]
        )
        for p in range(parts)
    ]
    for copy in copies:
        copy.start()
    sends = []
    wanted = wanted_rows(asked_ref[...])
    for kind in range(3):
        wanted_ref[kind] = wanted[kind]
    token = (iota((ROWS, 128), 0) + 1).astype(F32)
    lane_head = (iota((ROWS, 128), 1) >> 2) & 1
    for s in range(SEQ):
        peers = slice(s * GRP, (s + 1) * GRP)
        high_match = wanted[2][s : s + 1, :] == token
        high = jnp.zeros((128, 3 * HEAD), F32)
        if s % share == 0:
            copies[s // share].wait()
        for h in range(2):
            start = (2 * (s % share) + h) * HEAD
            packed = jnp.concatenate(
                [qkv_ref[s // share, c, :, start : start + HEAD] for c in range(3)], axis=1
            )
            low_match = jnp.where(wanted[h][s : s + 1, :] == token, 1.0, 0.0).astype(BF16)
            low = dot(low_match, packed, TN).astype(BF16)
            mine = jnp.where(high_match & (lane_head == h), 1.0, 0.0).astype(BF16)
            high = high + dot(mine, packed, TN)
            for c in range(3):
                out_ref[peers, h * 3 + c] = low[:, c * HEAD : (c + 1) * HEAD].reshape(GRP, 8, HEAD)
        high = high.astype(BF16)
        for c in range(3):
            out_ref[peers, 6 + c] = high[:, c * HEAD : (c + 1) * HEAD].reshape(GRP, 8, HEAD)
        if s % 2 == 1:
            span = pl.ds((s - 1) * GRP, 2 * GRP)
            sends.append(
                pltpu.make_async_copy(out_ref.at[span], out_hbm.at[span], out_sems.at[s // 2])
            )
            sends[-1].start()
    for send in sends:
        send.wait()


def attend_kernel(empty_ref, x_ref, out_ref, packed_ref, causal_ref, result_ref):
    factor = HEAD ** (-0.5) * 1.4426950408889634
    low_rows = GROUP * LOW
    high_rows = GROUP * HIGH
    joint = iota((2 * high_rows, high_rows), 0)
    apart = iota((2 * high_rows, high_rows), 1)
    same_place = (joint >> 3) * HIGH + (joint & 3) == apart
    spread = [
        jnp.where(same_place & (((joint >> 2) & 1) == h), 1.0, 0.0).astype(BF16) for h in range(2)
    ]

    def order_of(index):
        source, slot = place_order(index)
        return source * SLOTS + slot

    later = order_of(iota((1, GROWS), 1)) > order_of(iota((GROWS, 1), 0))
    causal_ref[...] = jnp.where(later, FAR, 0.0)
    groups = DEVICES // GROUP
    for i in range(groups):
        blocks = slice(i * GROUP, (i + 1) * GROUP)
        start, stop = i * GROWS, (i + 1) * GROWS
        for c in range(3):
            both = x_ref[blocks, 6 + c].reshape(2 * high_rows, HEAD)
            for h in range(2):
                packed_ref[h, c, start : start + low_rows, :] = x_ref[blocks, h * 3 + c].reshape(
                    low_rows, HEAD
                )
                packed_ref[h, c, start + low_rows : stop, :] = dot(spread[h], both, TN).astype(BF16)

    piece = GROWS // PIECES

    def score(i, h, q):
        start, stop = i * GROWS, (i + 1) * GROWS
        inner = slice(q * piece, (q + 1) * piece)
        queries = packed_ref[h, 0, start + q * piece : start + (q + 1) * piece, :]
        near = dot(queries, packed_ref[h, 1, start:stop, :], NT)
        near = near + causal_ref[inner, :] + empty_ref[h, 0:1, start:stop]
        if i == 0:
            return (near,)
        far = dot(queries, packed_ref[h, 1, :start, :], NT) + empty_ref[h, 0:1, :start]
        return (near, far)

    def finish(i, h, q, scores):
        start, stop = i * GROWS, (i + 1) * GROWS
        top = jnp.max(scores[0], axis=1, keepdims=True)
        for part in scores[1:]:
            top = jnp.maximum(top, jnp.max(part, axis=1, keepdims=True))
        summed = jnp.zeros((piece, 2 * HEAD), F32)
        for part, (begin, end) in zip(scores, ((start, stop), (0, start))):
            weights = jnp.exp2((part - top) * factor).astype(BF16)
            values = jnp.concatenate(
                [packed_ref[h, 2, begin:end, :], jnp.ones((end - begin, 128), BF16)], axis=1
            )
            summed = summed + dot(weights, values)
        result_ref[q * piece : (q + 1) * piece, :] = (summed[:, :HEAD] / summed[:, HEAD:]).astype(BF16)

    steps = [(i, h, q) for i in range(groups) for h in range(2) for q in range(PIECES)]
    ready = score(*steps[0])
    joined = None
    for n, (i, h, q) in enumerate(steps):
        scores = ready
        if n + 1 < len(steps):
            ready = score(*steps[n + 1])
        finish(i, h, q, scores)
        if q < PIECES - 1:
            continue
        blocks = slice(i * GROUP, (i + 1) * GROUP)
        out_ref[blocks, h] = result_ref[:low_rows].reshape(GROUP, 8, HEAD)
        part = dot(spread[h], result_ref[low_rows:])
        joined = part if h == 0 else joined + part
        if h == 1:
            out_ref[blocks, 2] = joined.astype(BF16).reshape(GROUP, 8, HEAD)


def mix_kernel(
    rows_ref, wanted_ref, came_ref, w_out_ref, gain_ref, mixed_ref, out_hbm,
    w_ref, att_ref, tall_ref, tile_ref, out_ref, w_sems, out_sems,
):
    parts = w_sems.shape[0]
    span = WIDTH // parts
    copies = [
        pltpu.make_async_copy(w_out_ref.at[:, pl.ds(p * span, span)], w_ref.at[p], w_sems.at[p])
        for p in range(parts)
    ]
    for copy in copies:
        copy.start()
    token = (iota((ROWS, 128), 0) + 1).astype(F32)
    lane_head = (iota((ROWS, 128), 1) >> 2) & 1
    for s in range(SEQ):
        peers = slice(s * GRP, (s + 1) * GRP)
        high_match = wanted_ref[2, s : s + 1, :] == token
        high = came_ref[peers, 2].reshape(128, HEAD)
        for h in range(2):
            low_match = jnp.where(wanted_ref[h, s : s + 1, :] == token, 1.0, 0.0).astype(BF16)
            mine = jnp.where(high_match & (lane_head == h), 1.0, 0.0).astype(BF16)
            got = dot(
                jnp.concatenate([low_match, mine], axis=1),
                jnp.concatenate([came_ref[peers, h].reshape(128, HEAD), high], axis=0),
            )
            start = (2 * s + h) * HEAD
            att_ref[:, start : start + HEAD] = got.astype(BF16)
    attended = att_ref[...]
    for p in range(parts):
        copies[p].wait()
        mixed_ref[:, p * span : (p + 1) * span] = dot(attended, w_ref[p]).astype(BF16)
    wide = mixed_ref[...].astype(F32)
    mean_square = jnp.mean(wide * wide, axis=1, keepdims=True)
    normed = wide * lax.rsqrt(mean_square + 1e-06) * gain_ref[...].astype(F32)
    for j in range(CHUNKS):
        tall_ref[pl.ds(j, ROWS, stride=PITCH), :] = normed[:, j * 128 : (j + 1) * 128]
    for t in range(ROWS):
        tile_ref[t] = tall_ref[t * PITCH : t * PITCH + CHUNKS, :].astype(BF16)
    sends = out_sems.shape[0]
    share = DEVICES // sends
    outs = []
    for p in range(sends):
        for e in range(p * share, (p + 1) * share):
            for k in range(ESLOTS):
                out_ref[e * ESLOTS + k] = tile_ref[rows_ref[k, e]]
        span = pl.ds(p * share * ESLOTS, share * ESLOTS)
        outs.append(pltpu.make_async_copy(out_ref.at[span], out_hbm.at[span], out_sems.at[p]))
        outs[-1].start()
    for copy in outs:
        copy.wait()


def expert_kernel(
    place_ref, slots_ref, x_ref, gate_hbm, up_hbm, down_hbm, router_ref, out_hbm,
    out_ref, gate_ref, up_ref, down_ref, tall_ref, rows_ref, hidden_ref, sems, send_sems,
):
    copies = [
        pltpu.make_async_copy(source.at[0], target, sems.at[n])
        for n, (source, target) in enumerate(
            [(gate_hbm, gate_ref), (up_hbm, up_ref), (down_hbm, down_ref)]
        )
    ]
    for copy in copies:
        copy.start()
    me = place_ref[0]
    for i in range(CHOSEN):
        tall_ref[i * PITCH : i * PITCH + CHUNKS, :] = x_ref[slots_ref[0, i]].astype(F32)
    for j in range(CHUNKS):
        rows_ref[:, j * 128 : (j + 1) * 128] = tall_ref[pl.ds(j, CHOSEN, stride=PITCH), :].astype(BF16)
    out_ref[...] = jnp.zeros(out_ref.shape, BF16)
    rows = rows_ref[...]
    wide = HIDDEN // 3
    for n in range(3):
        columns = slice(n * wide, (n + 1) * wide)
        if n == 0:
            copies[0].wait()
        gate = dot(rows, gate_ref[:, columns])
        if n == 0:
            copies[1].wait()
        up = dot(rows, up_ref[:, columns])
        hidden_ref[:, columns] = (jax.nn.silu(gate) * up).astype(BF16)
    logits = dot(rows, router_ref[...])
    mine = jnp.where(iota((CHOSEN, 128), 1) == me, logits, 0.0)
    weight = jax.nn.sigmoid(jnp.sum(mine, axis=1, keepdims=True))
    copies[2].wait()
    hidden = hidden_ref[...]
    for n in range(8):
        result = dot(hidden, down_ref[:, n * 256 : (n + 1) * 256]) * weight
        for j in range(2):
            tall_ref[pl.ds(2 * n + j, CHOSEN, stride=PITCH), :] = result[:, j * 128 : (j + 1) * 128]
    edges = (0, CHOSEN // 4, CHOSEN // 2, 3 * CHOSEN // 4, SENT)
    sends = []
    for p in range(4):
        for i in range(p * CHOSEN // 4, (p + 1) * CHOSEN // 4):
            out_ref[slots_ref[0, i]] = tall_ref[i * PITCH : i * PITCH + CHUNKS, :].astype(BF16)
        span = pl.ds(edges[p], edges[p + 1] - edges[p])
        sends.append(pltpu.make_async_copy(out_ref.at[span], out_hbm.at[span], send_sems.at[p]))
        sends[-1].start()
    for send in sends:
        send.wait()


def combine_kernel(marks_ref, mixed_ref, x_ref, out_ref, tall_ref):
    for e in range(DEVICES):
        for k in range(ESLOTS):
            start = (k * DEVICES + e) * PITCH
            tall_ref[start : start + CHUNKS, :] = x_ref[e * ESLOTS + k].astype(F32)
    token = iota((ROWS, DEVICES), 0) + 1
    match = jnp.concatenate(
        [jnp.where(marks_ref[k : k + 1, :] == token, 1.0, 0.0) for k in range(ESLOTS)], axis=1
    ).astype(BF16)
    for n in range(CHUNKS // 2):
        flat = jnp.concatenate(
            [
                tall_ref[pl.ds(2 * n + j, SENT, stride=PITCH), :].astype(BF16)
                for j in range(2)
            ],
            axis=1,
        )
        columns = slice(n * 256, (n + 1) * 256)
        out_ref[:, columns] = (mixed_ref[:, columns].astype(F32) + dot(match, flat)).astype(BF16)


def call(kernel, out_shape, in_specs, scratch=(), out_specs=None):
    return pl.pallas_call(
        kernel,
        out_shape=out_shape,
        in_specs=in_specs,
        out_specs=jax.tree.map(lambda _: whole(), out_shape) if out_specs is None else out_specs,
        scratch_shapes=list(scratch),
        compiler_params=pltpu.CompilerParams(vmem_limit_bytes=VMEM_LIMIT),
    )


def shape(dims, dtype=BF16):
    return jax.ShapeDtypeStruct(dims, dtype)


def exchange(array):
    return lax.all_to_all(array, ALL, split_axis=0, concat_axis=0, tiled=True)


def near(array):
    return pltpu.with_memory_space_constraint(array, pltpu.VMEM)


def shards(qkv, cluster_lists, w_out, norm_gain, router, expert_lists, w_gate, w_up, w_down):
    me = lax.axis_index("seq") * GRP + lax.axis_index("grp")
    place = me.reshape(1).astype(I32)
    smem = whole(pltpu.SMEM)
    hbm = whole(pl.ANY)

    request = call(request_kernel, shape((DEVICES, 128), F32), [whole()])(cluster_lists)
    asked = exchange(request.reshape(DEVICES, 1, 128)).reshape(DEVICES, 128)
    empty = call(empty_kernel, shape((2, 8, PLACES), F32), [whole()])(cluster_lists)
    marks, rows, slots = call(
        expert_index_kernel,
        (shape((8, DEVICES), I32), shape((8, DEVICES), I32), shape((1, CHOSEN), I32)),
        [smem, whole()],
    )(place, expert_lists)

    wanted, picked = call(
        select_kernel,
        (shape((3, SEQ, 128), F32), shape((DEVICES, 9, 8, HEAD))),
        [whole(), hbm],
        [
            pltpu.VMEM((2, 3, ROWS, WIDTH // 2), BF16),
            pltpu.VMEM((DEVICES, 9, 8, HEAD), BF16),
            pltpu.SemaphoreType.DMA((2,)),
            pltpu.SemaphoreType.DMA((4,)),
        ],
        out_specs=(whole(), hbm),
    )(asked, qkv.transpose(1, 0, 2))
    arrived = exchange(picked)

    outputs = call(
        attend_kernel,
        shape((DEVICES, 3, 8, HEAD)),
        [whole(), whole()],
        [
            pltpu.VMEM((2, 3, PLACES, HEAD), BF16),
            pltpu.VMEM((GROWS, GROWS), F32),
            pltpu.VMEM((GROWS, HEAD), BF16),
        ],
    )(empty, near(arrived))
    came_back = exchange(outputs)

    mixed, outgoing = call(
        mix_kernel,
        (shape((ROWS, WIDTH)), shape((SENT, CHUNKS, 128))),
        [smem, whole(), whole(), hbm, whole()],
        [
            pltpu.VMEM((4, WIDTH, WIDTH // 4), BF16),
            pltpu.VMEM((ROWS, WIDTH), BF16),
            pltpu.VMEM((ROWS * PITCH, 128), F32),
            pltpu.VMEM((ROWS, CHUNKS, 128), BF16),
            pltpu.VMEM((SENT, CHUNKS, 128), BF16),
            pltpu.SemaphoreType.DMA((4,)),
            pltpu.SemaphoreType.DMA((4,)),
        ],
        out_specs=(whole(), hbm),
    )(rows, wanted, near(came_back), w_out, norm_gain.reshape(1, WIDTH))
    incoming = exchange(outgoing)

    produced = call(
        expert_kernel,
        shape((SENT, CHUNKS, 128)),
        [smem, smem, whole(), hbm, hbm, hbm, whole()],
        [
            pltpu.VMEM((SENT, CHUNKS, 128), BF16),
            pltpu.VMEM((WIDTH, HIDDEN), BF16),
            pltpu.VMEM((WIDTH, HIDDEN), BF16),
            pltpu.VMEM((HIDDEN, WIDTH), BF16),
            pltpu.VMEM((CHOSEN * PITCH, 128), F32),
            pltpu.VMEM((CHOSEN, WIDTH), BF16),
            pltpu.VMEM((CHOSEN, HIDDEN), BF16),
            pltpu.SemaphoreType.DMA((3,)),
            pltpu.SemaphoreType.DMA((4,)),
        ],
        out_specs=hbm,
    )(place, slots, near(incoming), w_gate, w_up, w_down, router)
    results = exchange(produced)

    return call(
        combine_kernel,
        shape((ROWS, WIDTH)),
        [whole(), whole(), whole()],
        [pltpu.VMEM((SENT * PITCH, 128), F32)],
    )(marks, mixed, near(results))


def solution(mesh):
    return jax.shard_map(
        shards,
        mesh=mesh,
        in_specs=(
            P(("seq", "grp"), None, None),
            P("seq", "grp", None),
            P(),
            P(),
            P(),
            P(),
            P(("seq", "grp"), None, None),
            P(("seq", "grp"), None, None),
            P(("seq", "grp"), None, None),
        ),
        out_specs=P(("seq", "grp"), None),
        check_vma=False,
    )
```

```python
import jax
import jax.numpy as jnp
from jax import lax
from jax.experimental import pallas as pl
from jax.experimental.pallas import tpu as pltpu
from jax.sharding import PartitionSpec as P

BF16 = jnp.bfloat16
F32 = jnp.float32
I32 = jnp.int32
ALL = ("seq", "grp")

SEQ = 8
GRP = 16
DEVICES = 128
ROWS = 128
HEAD = 128
WIDTH = 2048
CHUNKS = WIDTH // 128
CLUSTER = 1024
SLOTS = 12
LOW = 8
HIGH = 4
ESLOTS = 6
CHOSEN = 512
HIDDEN = 768
SENT = DEVICES * ESLOTS
GROUP = 32
FAR = -1e30
PIECES = 3
EARLY = 512
PITCH = CHUNKS + 1
GROWS = GROUP * SLOTS
PLACES = DEVICES * SLOTS

NN = (((1,), (0,)), ((), ()))
NT = (((1,), (1,)), ((), ()))
TN = (((0,), (0,)), ((), ()))
VMEM_LIMIT = 60 * 1024 * 1024


def iota(shape, axis):
    return lax.broadcasted_iota(I32, shape, axis)


def dot(a, b, dims=NN):
    return lax.dot_general(a, b, dims, preferred_element_type=F32)


def whole(space=pltpu.VMEM):
    return pl.BlockSpec(memory_space=space)


def fetch(pairs, sems):
    copies = [pltpu.make_async_copy(a, b, sems.at[n]) for n, (a, b) in enumerate(pairs)]
    for copy in copies:
        copy.start()
    return copies


def rank_in_block(block, most):
    lane = iota(block.shape, 1)
    rank = jnp.zeros(block.shape, I32)
    for back in range(1, most):
        same = (pltpu.roll(block, back, 1) == block) & (lane >= back)
        rank = rank + jnp.where(same, 1, 0)
    return rank


def request_kernel(lists_ref, out_ref):
    line = iota((128, CLUSTER), 0)
    asked = jnp.zeros((DEVICES, 128), F32)
    for h in range(2):
        token = lists_ref[h]
        block = token >> 7
        slot_line = h * 16 + rank_in_block(block, SLOTS)
        row = ((token & 127) + 1).astype(F32)
        member = jnp.where(block == line, 1.0, 0.0).astype(BF16)
        rows = jnp.where(slot_line == line, row, 0.0).astype(BF16)
        asked = asked + dot(member, rows, NT)
    out_ref[...] = asked


def place_order(index):
    group = index // GROWS
    inner = index - group * GROWS
    upper = inner - GROUP * LOW
    is_low = inner < GROUP * LOW
    source = group * GROUP + jnp.where(is_low, inner >> 3, upper >> 2)
    slot = jnp.where(is_low, inner & 7, LOW + (upper & 3))
    return source, slot


def empty_kernel(lists_ref, out_ref):
    line = iota((128, CLUSTER), 0)
    source, slot = place_order(iota((1, PLACES), 1))
    spread = jnp.where(iota((128, PLACES), 0) == source, 1.0, 0.0).astype(BF16)
    for h in range(2):
        member = jnp.where((lists_ref[h] >> 7) == line, 1.0, 0.0).astype(BF16)
        count = dot(jnp.ones((8, CLUSTER), BF16), member, NT)
        held = dot(count.astype(BF16), spread)
        out_ref[h] = jnp.where(slot.astype(F32) < held, 0.0, FAR)


def expert_index_kernel(
    place_ref, lists_ref, w_out_hbm, marks_ref, rows_ref, slots_ref, early_ref, sem
):
    early = pltpu.make_async_copy(w_out_hbm.at[:, pl.ds(0, EARLY)], early_ref, sem)
    early.start()
    me = place_ref[0]
    lists = lists_ref[...]
    inside = (lists >> 7) == me
    position = iota((DEVICES, CHOSEN), 1)
    before = jnp.sum(jnp.where(lists < me * ROWS, 1.0, 0.0), axis=1, keepdims=True).astype(I32)
    row = (lists - me * ROWS + 1).astype(F32)
    rank = jnp.where(inside, position - before, -1)
    lane = iota((DEVICES, 128), 1)
    rows = jnp.zeros((DEVICES, 128), F32)
    for k in range(ESLOTS):
        found = jnp.sum(jnp.where(rank == k, row, 0.0), axis=1, keepdims=True)
        rows = jnp.where(lane == k, found, rows)
    marks = rows.T[:8].astype(I32)
    marks_ref[...] = marks
    rows_ref[...] = jnp.maximum(marks - 1, 0)
    mine = lists_ref[pl.ds(me, 1), :]
    block = mine >> 7
    slots_ref[...] = block * ESLOTS + rank_in_block(block, ESLOTS)
    early.wait()


def wanted_rows(asked):
    asked = asked.astype(BF16)
    line = iota((128, 128), 0)
    lane = iota((128, 128), 1)
    seq_of = jnp.where(iota((SEQ, 128), 1) >> 4 == iota((SEQ, 128), 0), 1.0, 0.0).astype(BF16)
    wanted = []
    for kind in range(3):
        slot = (lane & 7) + 16 * kind if kind < 2 else ((lane >> 2) & 1) * 16 + LOW + (lane & 3)
        placed = dot(asked, jnp.where(line == slot, 1.0, 0.0).astype(BF16))
        placed = jnp.where((line & 15) == lane >> 3, placed, 0.0).astype(BF16)
        wanted.append(dot(seq_of, placed))
    return wanted


def select_kernel(asked_ref, qkv_hbm, wanted_ref, out_ref, qkv_ref, sems):
    arrival = fetch([(qkv_hbm, qkv_ref)], sems)
    wanted = wanted_rows(asked_ref[...])
    for kind in range(3):
        wanted_ref[kind] = wanted[kind]
    arrival[0].wait()
    token = (iota((ROWS, 128), 0) + 1).astype(F32)
    lane_head = (iota((ROWS, 128), 1) >> 2) & 1
    for s in range(SEQ):
        peers = slice(s * GRP, (s + 1) * GRP)
        high_match = wanted[2][s : s + 1, :] == token
        high = jnp.zeros((128, 3 * HEAD), F32)
        for h in range(2):
            start = (2 * s + h) * HEAD
            packed = jnp.concatenate(
                [qkv_ref[c, :, start : start + HEAD] for c in range(3)], axis=1
            )
            low_match = jnp.where(wanted[h][s : s + 1, :] == token, 1.0, 0.0).astype(BF16)
            low = dot(low_match, packed, TN).astype(BF16)
            mine = jnp.where(high_match & (lane_head == h), 1.0, 0.0).astype(BF16)
            high = high + dot(mine, packed, TN)
            for c in range(3):
                out_ref[peers, h * 3 + c] = low[:, c * HEAD : (c + 1) * HEAD].reshape(GRP, 8, HEAD)
        high = high.astype(BF16)
        for c in range(3):
            out_ref[peers, 6 + c] = high[:, c * HEAD : (c + 1) * HEAD].reshape(GRP, 8, HEAD)


def attend_kernel(empty_ref, x_ref, out_ref, packed_ref, causal_ref, result_ref):
    factor = HEAD ** (-0.5) * 1.4426950408889634
    low_rows = GROUP * LOW
    high_rows = GROUP * HIGH
    joint = iota((2 * high_rows, high_rows), 0)
    apart = iota((2 * high_rows, high_rows), 1)
    same_place = (joint >> 3) * HIGH + (joint & 3) == apart
    spread = [
        jnp.where(same_place & (((joint >> 2) & 1) == h), 1.0, 0.0).astype(BF16) for h in range(2)
    ]

    def order_of(index):
        source, slot = place_order(index)
        return source * SLOTS + slot

    later = order_of(iota((1, GROWS), 1)) > order_of(iota((GROWS, 1), 0))
    causal_ref[...] = jnp.where(later, FAR, 0.0)
    groups = DEVICES // GROUP
    for i in range(groups):
        blocks = slice(i * GROUP, (i + 1) * GROUP)
        start, stop = i * GROWS, (i + 1) * GROWS
        for c in range(3):
            both = x_ref[blocks, 6 + c].reshape(2 * high_rows, HEAD)
            for h in range(2):
                packed_ref[h, c, start : start + low_rows, :] = x_ref[blocks, h * 3 + c].reshape(
                    low_rows, HEAD
                )
                packed_ref[h, c, start + low_rows : stop, :] = dot(spread[h], both, TN).astype(BF16)

    piece = GROWS // PIECES

    def score(i, h, q):
        start, stop = i * GROWS, (i + 1) * GROWS
        inner = slice(q * piece, (q + 1) * piece)
        queries = packed_ref[h, 0, start + q * piece : start + (q + 1) * piece, :]
        near = dot(queries, packed_ref[h, 1, start:stop, :], NT)
        near = near + causal_ref[inner, :] + empty_ref[h, 0:1, start:stop]
        if i == 0:
            return (near,)
        far = dot(queries, packed_ref[h, 1, :start, :], NT) + empty_ref[h, 0:1, :start]
        return (near, far)

    def finish(i, h, q, scores):
        start, stop = i * GROWS, (i + 1) * GROWS
        top = jnp.max(scores[0], axis=1, keepdims=True)
        for part in scores[1:]:
            top = jnp.maximum(top, jnp.max(part, axis=1, keepdims=True))
        summed = jnp.zeros((piece, 2 * HEAD), F32)
        for part, (begin, end) in zip(scores, ((start, stop), (0, start))):
            weights = jnp.exp2((part - top) * factor).astype(BF16)
            values = jnp.concatenate(
                [packed_ref[h, 2, begin:end, :], jnp.ones((end - begin, 128), BF16)], axis=1
            )
            summed = summed + dot(weights, values)
        result_ref[q * piece : (q + 1) * piece, :] = (summed[:, :HEAD] / summed[:, HEAD:]).astype(BF16)

    steps = [(i, h, q) for i in range(groups) for h in range(2) for q in range(PIECES)]
    ready = score(*steps[0])
    joined = None
    for n, (i, h, q) in enumerate(steps):
        scores = ready
        if n + 1 < len(steps):
            ready = score(*steps[n + 1])
        finish(i, h, q, scores)
        if q < PIECES - 1:
            continue
        blocks = slice(i * GROUP, (i + 1) * GROUP)
        out_ref[blocks, h] = result_ref[:low_rows].reshape(GROUP, 8, HEAD)
        part = dot(spread[h], result_ref[low_rows:])
        joined = part if h == 0 else joined + part
        if h == 1:
            out_ref[blocks, 2] = joined.astype(BF16).reshape(GROUP, 8, HEAD)


def mix_kernel(
    rows_hbm, wanted_hbm, came_ref, early_ref, w_out_ref, gain_hbm, mixed_ref, out_hbm,
    rows_ref, wanted_ref, gain_ref, w_ref, att_ref, tall_ref, tile_ref, out_ref, w_sems, out_sems, sems,
):
    parts = w_sems.shape[0]
    span = (WIDTH - EARLY) // parts
    copies = [
        pltpu.make_async_copy(
            w_out_ref.at[:, pl.ds(EARLY + p * span, span)], w_ref.at[p], w_sems.at[p]
        )
        for p in range(parts)
    ]
    for copy in copies:
        copy.start()
    small = fetch([(wanted_hbm, wanted_ref), (gain_hbm, gain_ref), (rows_hbm, rows_ref)], sems)
    small[0].wait()
    token = (iota((ROWS, 128), 0) + 1).astype(F32)
    lane_head = (iota((ROWS, 128), 1) >> 2) & 1
    for s in range(SEQ):
        peers = slice(s * GRP, (s + 1) * GRP)
        high_match = wanted_ref[2, s : s + 1, :] == token
        high = came_ref[peers, 2].reshape(128, HEAD)
        for h in range(2):
            low_match = jnp.where(wanted_ref[h, s : s + 1, :] == token, 1.0, 0.0).astype(BF16)
            mine = jnp.where(high_match & (lane_head == h), 1.0, 0.0).astype(BF16)
            got = dot(
                jnp.concatenate([low_match, mine], axis=1),
                jnp.concatenate([came_ref[peers, h].reshape(128, HEAD), high], axis=0),
            )
            start = (2 * s + h) * HEAD
            att_ref[:, start : start + HEAD] = got.astype(BF16)
    attended = att_ref[...]
    mixed_ref[:, :EARLY] = dot(attended, early_ref[...]).astype(BF16)
    for p in range(parts):
        copies[p].wait()
        mixed_ref[:, EARLY + p * span : EARLY + (p + 1) * span] = dot(attended, w_ref[p]).astype(BF16)
    small[1].wait()
    small[2].wait()
    wide = mixed_ref[...].astype(F32)
    mean_square = jnp.mean(wide * wide, axis=1, keepdims=True)
    normed = wide * lax.rsqrt(mean_square + 1e-06) * gain_ref[...].astype(F32)
    for j in range(CHUNKS):
        tall_ref[pl.ds(j, ROWS, stride=PITCH), :] = normed[:, j * 128 : (j + 1) * 128]
    for t in range(ROWS):
        tile_ref[t] = tall_ref[t * PITCH : t * PITCH + CHUNKS, :].astype(BF16)
    sends = out_sems.shape[0]
    share = DEVICES // sends
    outs = []
    for p in range(sends):
        for e in range(p * share, (p + 1) * share):
            for k in range(ESLOTS):
                out_ref[e * ESLOTS + k] = tile_ref[rows_ref[k, e]]
        span = pl.ds(p * share * ESLOTS, share * ESLOTS)
        outs.append(pltpu.make_async_copy(out_ref.at[span], out_hbm.at[span], out_sems.at[p]))
        outs[-1].start()
    for copy in outs:
        copy.wait()


def expert_kernel(
    place_hbm, slots_hbm, x_ref, gate_hbm, up_hbm, down_hbm, router_hbm, out_hbm,
    place_ref, slots_ref, router_ref, out_ref, gate_ref, up_ref, down_ref, tall_ref, rows_ref, hidden_ref, sems, send_sems, small_sems,
):
    wide = HIDDEN // 3
    gates, ups = (
        [
            pltpu.make_async_copy(
                source.at[0, :, pl.ds(n * wide, wide)], target.at[n], sems.at[first + n]
            )
            for n in range(3)
        ]
        for source, target, first in ((gate_hbm, gate_ref, 0), (up_hbm, up_ref, 3))
    )
    downs = pltpu.make_async_copy(down_hbm.at[0], down_ref, sems.at[6])
    gates[0].start()
    ups[0].start()
    small = fetch([(place_hbm, place_ref), (slots_hbm, slots_ref)], small_sems)
    late = pltpu.make_async_copy(router_hbm, router_ref, small_sems.at[2])
    for copy in small:
        copy.wait()
    me = place_ref[0]
    for i in range(CHOSEN):
        tall_ref[i * PITCH : i * PITCH + CHUNKS, :] = x_ref[slots_ref[0, i]].astype(F32)
    gates[1].start()
    ups[1].start()
    for j in range(CHUNKS):
        rows_ref[:, j * 128 : (j + 1) * 128] = tall_ref[pl.ds(j, CHOSEN, stride=PITCH), :].astype(BF16)
    gates[2].start()
    ups[2].start()
    out_ref[...] = jnp.zeros(out_ref.shape, BF16)
    downs.start()
    late.start()
    rows = rows_ref[...]
    for n in range(3):
        columns = slice(n * wide, (n + 1) * wide)
        for part in ((0,), (1, 2), ())[n]:
            gates[part].wait()
            ups[part].wait()
        gate = dot(rows, gate_ref[n])
        up = dot(rows, up_ref[n])
        hidden_ref[:, columns] = (jax.nn.silu(gate) * up).astype(BF16)
    late.wait()
    downs.wait()
    logits = dot(rows, router_ref[...])
    mine = jnp.where(iota((CHOSEN, 128), 1) == me, logits, 0.0)
    weight = jax.nn.sigmoid(jnp.sum(mine, axis=1, keepdims=True))
    hidden = hidden_ref[...]
    for n in range(8):
        result = dot(hidden, down_ref[:, n * 256 : (n + 1) * 256]) * weight
        for j in range(2):
            tall_ref[pl.ds(2 * n + j, CHOSEN, stride=PITCH), :] = result[:, j * 128 : (j + 1) * 128]
    edges = (0, CHOSEN // 4, CHOSEN // 2, 3 * CHOSEN // 4, SENT)
    sends = []
    for p in range(4):
        for i in range(p * CHOSEN // 4, (p + 1) * CHOSEN // 4):
            out_ref[slots_ref[0, i]] = tall_ref[i * PITCH : i * PITCH + CHUNKS, :].astype(BF16)
        span = pl.ds(edges[p], edges[p + 1] - edges[p])
        sends.append(pltpu.make_async_copy(out_ref.at[span], out_hbm.at[span], send_sems.at[p]))
        sends[-1].start()
    for send in sends:
        send.wait()


def combine_kernel(marks_hbm, mixed_hbm, x_ref, out_ref, tall_ref, marks_ref, mixed_ref, sems):
    small = fetch([(marks_hbm, marks_ref), (mixed_hbm, mixed_ref)], sems)
    for e in range(DEVICES):
        for k in range(ESLOTS):
            start = (k * DEVICES + e) * PITCH
            tall_ref[start : start + CHUNKS, :] = x_ref[e * ESLOTS + k].astype(F32)
    for copy in small:
        copy.wait()
    token = iota((ROWS, DEVICES), 0) + 1
    match = jnp.concatenate(
        [jnp.where(marks_ref[k : k + 1, :] == token, 1.0, 0.0) for k in range(ESLOTS)], axis=1
    ).astype(BF16)
    for n in range(CHUNKS // 2):
        flat = jnp.concatenate(
            [
                tall_ref[pl.ds(2 * n + j, SENT, stride=PITCH), :].astype(BF16)
                for j in range(2)
            ],
            axis=1,
        )
        columns = slice(n * 256, (n + 1) * 256)
        out_ref[:, columns] = (mixed_ref[:, columns].astype(F32) + dot(match, flat)).astype(BF16)


def specs_of(out_shape):
    return tuple(whole() for _ in out_shape) if isinstance(out_shape, tuple) else whole()


def call(kernel, out_shape, in_specs, scratch=(), out_specs=None):
    return pl.pallas_call(
        kernel,
        out_shape=out_shape,
        in_specs=in_specs,
        out_specs=specs_of(out_shape) if out_specs is None else out_specs,
        scratch_shapes=list(scratch),
        compiler_params=pltpu.CompilerParams(vmem_limit_bytes=VMEM_LIMIT),
    )


def shape(dims, dtype=BF16):
    return jax.ShapeDtypeStruct(dims, dtype)


def held(dims, dtype=BF16):
    return pltpu.VMEM(dims, dtype)


def exchange(array):
    return lax.all_to_all(array, ALL, split_axis=0, concat_axis=0, tiled=True)


def near(array):
    return pltpu.with_memory_space_constraint(array, pltpu.VMEM)


def shards(qkv, cluster_lists, w_out, norm_gain, router, expert_lists, w_gate, w_up, w_down):
    me = lax.axis_index("seq") * GRP + lax.axis_index("grp")
    place = me.reshape(1).astype(I32)
    smem = whole(pltpu.SMEM)
    hbm = whole(pl.ANY)

    request = call(request_kernel, held((DEVICES, 128), F32), [whole()])(cluster_lists)
    asked = exchange(request.reshape(DEVICES, 1, 128)).reshape(DEVICES, 128)
    empty = call(empty_kernel, shape((2, 8, PLACES), F32), [whole()])(cluster_lists)
    marks, rows, slots, early = call(
        expert_index_kernel,
        (
            shape((8, DEVICES), I32),
            shape((8, DEVICES), I32),
            shape((1, CHOSEN), I32),
            held((WIDTH, EARLY)),
        ),
        [smem, whole(), hbm],
        [pltpu.SemaphoreType.DMA(())],
    )(place, expert_lists, w_out)

    wanted, picked = call(
        select_kernel,
        (shape((3, SEQ, 128), F32), shape((DEVICES, 9, 8, HEAD))),
        [whole(), hbm],
        [pltpu.VMEM((3, ROWS, WIDTH), BF16), pltpu.SemaphoreType.DMA((1,))],
    )(near(asked), qkv.transpose(1, 0, 2))
    arrived = exchange(picked)

    outputs = call(
        attend_kernel,
        shape((DEVICES, 3, 8, HEAD)),
        [whole(), whole()],
        [
            pltpu.VMEM((2, 3, PLACES, HEAD), BF16),
            pltpu.VMEM((GROWS, GROWS), F32),
            pltpu.VMEM((GROWS, HEAD), BF16),
        ],
    )(empty, near(arrived))
    came_back = exchange(outputs)

    mixed, outgoing = call(
        mix_kernel,
        (shape((ROWS, WIDTH)), shape((SENT, CHUNKS, 128))),
        [hbm, hbm, whole(), whole(), hbm, hbm],
        [
            pltpu.SMEM((8, DEVICES), I32),
            pltpu.VMEM((3, SEQ, 128), F32),
            pltpu.VMEM((1, WIDTH), BF16),
            pltpu.VMEM((3, WIDTH, (WIDTH - EARLY) // 3), BF16),
            pltpu.VMEM((ROWS, WIDTH), BF16),
            pltpu.VMEM((ROWS * PITCH, 128), F32),
            pltpu.VMEM((ROWS, CHUNKS, 128), BF16),
            pltpu.VMEM((SENT, CHUNKS, 128), BF16),
            pltpu.SemaphoreType.DMA((3,)),
            pltpu.SemaphoreType.DMA((4,)),
            pltpu.SemaphoreType.DMA((3,)),
        ],
        out_specs=(whole(), hbm),
    )(rows, wanted, near(came_back), near(early), w_out, norm_gain.reshape(1, WIDTH))
    incoming = exchange(outgoing)

    produced = call(
        expert_kernel,
        shape((SENT, CHUNKS, 128)),
        [hbm, hbm, whole(), hbm, hbm, hbm, hbm],
        [
            pltpu.SMEM((1,), I32),
            pltpu.SMEM((1, CHOSEN), I32),
            pltpu.VMEM((WIDTH, 128), BF16),
            pltpu.VMEM((SENT, CHUNKS, 128), BF16),
            pltpu.VMEM((3, WIDTH, HIDDEN // 3), BF16),
            pltpu.VMEM((3, WIDTH, HIDDEN // 3), BF16),
            pltpu.VMEM((HIDDEN, WIDTH), BF16),
            pltpu.VMEM((CHOSEN * PITCH, 128), F32),
            pltpu.VMEM((CHOSEN, WIDTH), BF16),
            pltpu.VMEM((CHOSEN, HIDDEN), BF16),
            pltpu.SemaphoreType.DMA((7,)),
            pltpu.SemaphoreType.DMA((4,)),
            pltpu.SemaphoreType.DMA((3,)),
        ],
        out_specs=hbm,
    )(place, slots, near(incoming), w_gate, w_up, w_down, router)
    results = exchange(produced)

    return call(
        combine_kernel,
        shape((ROWS, WIDTH)),
        [hbm, hbm, whole()],
        [
            pltpu.VMEM((SENT * PITCH, 128), F32),
            pltpu.VMEM((8, DEVICES), I32),
            pltpu.VMEM((ROWS, WIDTH), BF16),
            pltpu.SemaphoreType.DMA((2,)),
        ],
    )(marks, mixed, near(results))


def solution(mesh):
    return jax.shard_map(
        shards,
        mesh=mesh,
        in_specs=(
            P(("seq", "grp"), None, None),
            P("seq", "grp", None),
            P(),
            P(),
            P(),
            P(),
            P(("seq", "grp"), None, None),
            P(("seq", "grp"), None, None),
            P(("seq", "grp"), None, None),
        ),
        out_specs=P(("seq", "grp"), None),
        check_vma=False,
    )
```

```python
import jax
import jax.numpy as jnp
from jax import lax
from jax.experimental import pallas as pl
from jax.experimental.pallas import tpu as pltpu
from jax.sharding import PartitionSpec as P

BF16 = jnp.bfloat16
F32 = jnp.float32
I32 = jnp.int32
ALL = ("seq", "grp")

SEQ = 8
GRP = 16
DEVICES = 128
ROWS = 128
HEAD = 128
WIDTH = 2048
CHUNKS = WIDTH // 128
CLUSTER = 1024
SLOTS = 12
LOW = 8
HIGH = 4
ESLOTS = 6
CHOSEN = 512
HIDDEN = 768
SENT = DEVICES * ESLOTS
GROUP = 32
FAR = -1e30
PIECES = 3
EARLY = 512
PITCH = CHUNKS + 1
GROWS = GROUP * SLOTS
PLACES = DEVICES * SLOTS

NN = (((1,), (0,)), ((), ()))
NT = (((1,), (1,)), ((), ()))
TN = (((0,), (0,)), ((), ()))
VMEM_LIMIT = 60 * 1024 * 1024


def iota(shape, axis):
    return lax.broadcasted_iota(I32, shape, axis)


def dot(a, b, dims=NN):
    return lax.dot_general(a, b, dims, preferred_element_type=F32)


def whole(space=pltpu.VMEM):
    return pl.BlockSpec(memory_space=space)


def fetch(pairs, sems):
    copies = [pltpu.make_async_copy(a, b, sems.at[n]) for n, (a, b) in enumerate(pairs)]
    for copy in copies:
        copy.start()
    return copies


def rank_in_block(block, most):
    lane = iota(block.shape, 1)
    rank = jnp.zeros(block.shape, I32)
    for back in range(1, most):
        same = (pltpu.roll(block, back, 1) == block) & (lane >= back)
        rank = rank + jnp.where(same, 1, 0)
    return rank


def request_kernel(lists_ref, out_ref):
    line = iota((128, CLUSTER), 0)
    asked = jnp.zeros((DEVICES, 128), F32)
    for h in range(2):
        token = lists_ref[h]
        block = token >> 7
        slot_line = h * 16 + rank_in_block(block, SLOTS)
        row = ((token & 127) + 1).astype(F32)
        member = jnp.where(block == line, 1.0, 0.0).astype(BF16)
        rows = jnp.where(slot_line == line, row, 0.0).astype(BF16)
        asked = asked + dot(member, rows, NT)
    out_ref[...] = asked


def place_order(index):
    group = index // GROWS
    inner = index - group * GROWS
    upper = inner - GROUP * LOW
    is_low = inner < GROUP * LOW
    source = group * GROUP + jnp.where(is_low, inner >> 3, upper >> 2)
    slot = jnp.where(is_low, inner & 7, LOW + (upper & 3))
    return source, slot


def empty_kernel(lists_ref, out_ref):
    line = iota((128, CLUSTER), 0)
    source, slot = place_order(iota((1, PLACES), 1))
    spread = jnp.where(iota((128, PLACES), 0) == source, 1.0, 0.0).astype(BF16)
    for h in range(2):
        member = jnp.where((lists_ref[h] >> 7) == line, 1.0, 0.0).astype(BF16)
        count = dot(jnp.ones((8, CLUSTER), BF16), member, NT)
        held = dot(count.astype(BF16), spread)
        out_ref[h] = jnp.where(slot.astype(F32) < held, 0.0, FAR)


def expert_index_kernel(
    place_ref, lists_ref, w_out_hbm, marks_ref, rows_ref, slots_ref, early_ref, sem
):
    early = pltpu.make_async_copy(w_out_hbm.at[:, pl.ds(0, EARLY)], early_ref, sem)
    early.start()
    me = place_ref[0]
    lists = lists_ref[...]
    inside = (lists >> 7) == me
    position = iota((DEVICES, CHOSEN), 1)
    before = jnp.sum(jnp.where(lists < me * ROWS, 1.0, 0.0), axis=1, keepdims=True).astype(I32)
    row = (lists - me * ROWS + 1).astype(F32)
    rank = jnp.where(inside, position - before, -1)
    lane = iota((DEVICES, 128), 1)
    rows = jnp.zeros((DEVICES, 128), F32)
    for k in range(ESLOTS):
        found = jnp.sum(jnp.where(rank == k, row, 0.0), axis=1, keepdims=True)
        rows = jnp.where(lane == k, found, rows)
    marks = rows.T[:8].astype(I32)
    marks_ref[...] = marks
    rows_ref[...] = jnp.maximum(marks - 1, 0)
    mine = lists_ref[pl.ds(me, 1), :]
    block = mine >> 7
    slots_ref[...] = block * ESLOTS + rank_in_block(block, ESLOTS)
    early.wait()


def wanted_rows(asked):
    asked = asked.astype(BF16)
    line = iota((128, 128), 0)
    lane = iota((128, 128), 1)
    seq_of = jnp.where(iota((SEQ, 128), 1) >> 4 == iota((SEQ, 128), 0), 1.0, 0.0).astype(BF16)
    wanted = []
    for kind in range(3):
        slot = (lane & 7) + 16 * kind if kind < 2 else ((lane >> 2) & 1) * 16 + LOW + (lane & 3)
        placed = dot(asked, jnp.where(line == slot, 1.0, 0.0).astype(BF16))
        placed = jnp.where((line & 15) == lane >> 3, placed, 0.0).astype(BF16)
        wanted.append(dot(seq_of, placed))
    return wanted


def select_kernel(asked_ref, qkv_hbm, wanted_ref, out_ref, qkv_ref, sems):
    arrival = fetch([(qkv_hbm, qkv_ref)], sems)
    wanted = wanted_rows(asked_ref[...])
    for kind in range(3):
        wanted_ref[kind] = wanted[kind]
    arrival[0].wait()
    token = (iota((ROWS, 128), 0) + 1).astype(F32)
    lane_head = (iota((ROWS, 128), 1) >> 2) & 1
    for s in range(SEQ):
        peers = slice(s * GRP, (s + 1) * GRP)
        high_match = wanted[2][s : s + 1, :] == token
        high = jnp.zeros((128, 3 * HEAD), F32)
        for h in range(2):
            start = (2 * s + h) * HEAD
            packed = jnp.concatenate(
                [qkv_ref[c, :, start : start + HEAD] for c in range(3)], axis=1
            )
            low_match = jnp.where(wanted[h][s : s + 1, :] == token, 1.0, 0.0).astype(BF16)
            low = dot(low_match, packed, TN).astype(BF16)
            mine = jnp.where(high_match & (lane_head == h), 1.0, 0.0).astype(BF16)
            high = high + dot(mine, packed, TN)
            for c in range(3):
                out_ref[peers, h * 3 + c] = low[:, c * HEAD : (c + 1) * HEAD].reshape(GRP, 8, HEAD)
        high = high.astype(BF16)
        for c in range(3):
            out_ref[peers, 6 + c] = high[:, c * HEAD : (c + 1) * HEAD].reshape(GRP, 8, HEAD)


def attend_kernel(empty_ref, x_ref, out_ref, packed_ref, causal_ref, result_ref):
    factor = HEAD ** (-0.5) * 1.4426950408889634
    low_rows = GROUP * LOW
    high_rows = GROUP * HIGH
    joint = iota((2 * high_rows, high_rows), 0)
    apart = iota((2 * high_rows, high_rows), 1)
    same_place = (joint >> 3) * HIGH + (joint & 3) == apart
    spread = [
        jnp.where(same_place & (((joint >> 2) & 1) == h), 1.0, 0.0).astype(BF16) for h in range(2)
    ]

    def order_of(index):
        source, slot = place_order(index)
        return source * SLOTS + slot

    later = order_of(iota((1, GROWS), 1)) > order_of(iota((GROWS, 1), 0))
    causal_ref[...] = jnp.where(later, FAR, 0.0)
    groups = DEVICES // GROUP
    for i in range(groups):
        blocks = slice(i * GROUP, (i + 1) * GROUP)
        start, stop = i * GROWS, (i + 1) * GROWS
        for c in range(3):
            both = x_ref[blocks, 6 + c].reshape(2 * high_rows, HEAD)
            for h in range(2):
                packed_ref[h, c, start : start + low_rows, :] = x_ref[blocks, h * 3 + c].reshape(
                    low_rows, HEAD
                )
                packed_ref[h, c, start + low_rows : stop, :] = dot(spread[h], both, TN).astype(BF16)

    piece = GROWS // PIECES

    def score(i, h, q):
        start, stop = i * GROWS, (i + 1) * GROWS
        inner = slice(q * piece, (q + 1) * piece)
        queries = packed_ref[h, 0, start + q * piece : start + (q + 1) * piece, :]
        near = dot(queries, packed_ref[h, 1, start:stop, :], NT)
        near = near + causal_ref[inner, :] + empty_ref[h, 0:1, start:stop]
        if i == 0:
            return (near,)
        far = dot(queries, packed_ref[h, 1, :start, :], NT) + empty_ref[h, 0:1, :start]
        return (near, far)

    def finish(i, h, q, scores):
        start, stop = i * GROWS, (i + 1) * GROWS
        top = jnp.max(scores[0], axis=1, keepdims=True)
        for part in scores[1:]:
            top = jnp.maximum(top, jnp.max(part, axis=1, keepdims=True))
        summed = jnp.zeros((piece, 2 * HEAD), F32)
        for part, (begin, end) in zip(scores, ((start, stop), (0, start))):
            weights = jnp.exp2((part - top) * factor).astype(BF16)
            values = jnp.concatenate(
                [packed_ref[h, 2, begin:end, :], jnp.ones((end - begin, 128), BF16)], axis=1
            )
            summed = summed + dot(weights, values)
        result_ref[q * piece : (q + 1) * piece, :] = (summed[:, :HEAD] / summed[:, HEAD:]).astype(BF16)

    steps = [(i, h, q) for i in range(groups) for h in range(2) for q in range(PIECES)]
    ready = score(*steps[0])
    joined = None
    for n, (i, h, q) in enumerate(steps):
        scores = ready
        if n + 1 < len(steps):
            ready = score(*steps[n + 1])
        finish(i, h, q, scores)
        if q < PIECES - 1:
            continue
        blocks = slice(i * GROUP, (i + 1) * GROUP)
        out_ref[blocks, h] = result_ref[:low_rows].reshape(GROUP, 8, HEAD)
        part = dot(spread[h], result_ref[low_rows:])
        joined = part if h == 0 else joined + part
        if h == 1:
            out_ref[blocks, 2] = joined.astype(BF16).reshape(GROUP, 8, HEAD)


def mix_kernel(
    rows_hbm, wanted_hbm, came_ref, early_ref, w_out_ref, gain_hbm, mixed_ref, out_ref,
    rows_ref, wanted_ref, gain_ref, w_ref, att_ref, tall_ref, tile_ref, w_sems, sems,
):
    parts = w_sems.shape[0]
    span = (WIDTH - EARLY) // parts
    copies = [
        pltpu.make_async_copy(
            w_out_ref.at[:, pl.ds(EARLY + p * span, span)], w_ref.at[p], w_sems.at[p]
        )
        for p in range(parts)
    ]
    for copy in copies:
        copy.start()
    small = fetch([(wanted_hbm, wanted_ref), (gain_hbm, gain_ref), (rows_hbm, rows_ref)], sems)
    small[0].wait()
    token = (iota((ROWS, 128), 0) + 1).astype(F32)
    lane_head = (iota((ROWS, 128), 1) >> 2) & 1
    for s in range(SEQ):
        peers = slice(s * GRP, (s + 1) * GRP)
        high_match = wanted_ref[2, s : s + 1, :] == token
        high = came_ref[peers, 2].reshape(128, HEAD)
        for h in range(2):
            low_match = jnp.where(wanted_ref[h, s : s + 1, :] == token, 1.0, 0.0).astype(BF16)
            mine = jnp.where(high_match & (lane_head == h), 1.0, 0.0).astype(BF16)
            got = dot(
                jnp.concatenate([low_match, mine], axis=1),
                jnp.concatenate([came_ref[peers, h].reshape(128, HEAD), high], axis=0),
            )
            start = (2 * s + h) * HEAD
            att_ref[:, start : start + HEAD] = got.astype(BF16)
    attended = att_ref[...]
    mixed_ref[:, :EARLY] = dot(attended, early_ref[...]).astype(BF16)
    for p in range(parts):
        copies[p].wait()
        mixed_ref[:, EARLY + p * span : EARLY + (p + 1) * span] = dot(attended, w_ref[p]).astype(BF16)
    small[1].wait()
    small[2].wait()
    wide = mixed_ref[...].astype(F32)
    mean_square = jnp.mean(wide * wide, axis=1, keepdims=True)
    normed = wide * lax.rsqrt(mean_square + 1e-06) * gain_ref[...].astype(F32)
    for j in range(CHUNKS):
        tall_ref[pl.ds(j, ROWS, stride=PITCH), :] = normed[:, j * 128 : (j + 1) * 128]
    for t in range(ROWS):
        tile_ref[t] = tall_ref[t * PITCH : t * PITCH + CHUNKS, :].astype(BF16)
    for e in range(DEVICES):
        for k in range(ESLOTS):
            out_ref[e * ESLOTS + k] = tile_ref[rows_ref[k, e]]


def expert_kernel(
    place_hbm, slots_hbm, x_ref, gate_hbm, up_hbm, down_hbm, router_hbm, out_hbm,
    place_ref, slots_ref, router_ref, out_ref, gate_ref, up_ref, down_ref, tall_ref, rows_ref, hidden_ref, sems, send_sems, small_sems,
):
    wide = HIDDEN // 3
    gates, ups = (
        [
            pltpu.make_async_copy(
                source.at[0, :, pl.ds(n * wide, wide)], target.at[n], sems.at[first + n]
            )
            for n in range(3)
        ]
        for source, target, first in ((gate_hbm, gate_ref, 0), (up_hbm, up_ref, 3))
    )
    downs = pltpu.make_async_copy(down_hbm.at[0], down_ref, sems.at[6])
    gates[0].start()
    ups[0].start()
    small = fetch([(place_hbm, place_ref), (slots_hbm, slots_ref)], small_sems)
    late = pltpu.make_async_copy(router_hbm, router_ref, small_sems.at[2])
    for copy in small:
        copy.wait()
    me = place_ref[0]
    for i in range(CHOSEN):
        tall_ref[i * PITCH : i * PITCH + CHUNKS, :] = x_ref[slots_ref[0, i]].astype(F32)
    gates[1].start()
    ups[1].start()
    for j in range(CHUNKS):
        rows_ref[:, j * 128 : (j + 1) * 128] = tall_ref[pl.ds(j, CHOSEN, stride=PITCH), :].astype(BF16)
    gates[2].start()
    ups[2].start()
    out_ref[...] = jnp.zeros(out_ref.shape, BF16)
    downs.start()
    late.start()
    rows = rows_ref[...]
    for n in range(3):
        columns = slice(n * wide, (n + 1) * wide)
        for part in ((0,), (1, 2), ())[n]:
            gates[part].wait()
            ups[part].wait()
        gate = dot(rows, gate_ref[n])
        up = dot(rows, up_ref[n])
        hidden_ref[:, columns] = (jax.nn.silu(gate) * up).astype(BF16)
    late.wait()
    downs.wait()
    logits = dot(rows, router_ref[...])
    mine = jnp.where(iota((CHOSEN, 128), 1) == me, logits, 0.0)
    weight = jax.nn.sigmoid(jnp.sum(mine, axis=1, keepdims=True))
    hidden = hidden_ref[...]
    for n in range(8):
        result = dot(hidden, down_ref[:, n * 256 : (n + 1) * 256]) * weight
        for j in range(2):
            tall_ref[pl.ds(2 * n + j, CHOSEN, stride=PITCH), :] = result[:, j * 128 : (j + 1) * 128]
    edges = (0, CHOSEN // 4, CHOSEN // 2, 3 * CHOSEN // 4, SENT)
    sends = []
    for p in range(4):
        for i in range(p * CHOSEN // 4, (p + 1) * CHOSEN // 4):
            out_ref[slots_ref[0, i]] = tall_ref[i * PITCH : i * PITCH + CHUNKS, :].astype(BF16)
        span = pl.ds(edges[p], edges[p + 1] - edges[p])
        sends.append(pltpu.make_async_copy(out_ref.at[span], out_hbm.at[span], send_sems.at[p]))
        sends[-1].start()
    for send in sends:
        send.wait()


def combine_kernel(marks_hbm, mixed_hbm, x_ref, out_ref, tall_ref, marks_ref, mixed_ref, sems):
    small = fetch([(marks_hbm, marks_ref), (mixed_hbm, mixed_ref)], sems)
    for e in range(DEVICES):
        for k in range(ESLOTS):
            start = (k * DEVICES + e) * PITCH
            tall_ref[start : start + CHUNKS, :] = x_ref[e * ESLOTS + k].astype(F32)
    for copy in small:
        copy.wait()
    token = iota((ROWS, DEVICES), 0) + 1
    match = jnp.concatenate(
        [jnp.where(marks_ref[k : k + 1, :] == token, 1.0, 0.0) for k in range(ESLOTS)], axis=1
    ).astype(BF16)
    for n in range(CHUNKS // 2):
        flat = jnp.concatenate(
            [
                tall_ref[pl.ds(2 * n + j, SENT, stride=PITCH), :].astype(BF16)
                for j in range(2)
            ],
            axis=1,
        )
        columns = slice(n * 256, (n + 1) * 256)
        out_ref[:, columns] = (mixed_ref[:, columns].astype(F32) + dot(match, flat)).astype(BF16)


def specs_of(out_shape):
    return tuple(whole() for _ in out_shape) if isinstance(out_shape, tuple) else whole()


def call(kernel, out_shape, in_specs, scratch=(), out_specs=None):
    return pl.pallas_call(
        kernel,
        out_shape=out_shape,
        in_specs=in_specs,
        out_specs=specs_of(out_shape) if out_specs is None else out_specs,
        scratch_shapes=list(scratch),
        compiler_params=pltpu.CompilerParams(vmem_limit_bytes=VMEM_LIMIT),
    )


def shape(dims, dtype=BF16):
    return jax.ShapeDtypeStruct(dims, dtype)


def held(dims, dtype=BF16):
    return pltpu.VMEM(dims, dtype)


def exchange(array):
    return lax.all_to_all(array, ALL, split_axis=0, concat_axis=0, tiled=True)


def near(array):
    return pltpu.with_memory_space_constraint(array, pltpu.VMEM)


def shards(qkv, cluster_lists, w_out, norm_gain, router, expert_lists, w_gate, w_up, w_down):
    me = lax.axis_index("seq") * GRP + lax.axis_index("grp")
    place = me.reshape(1).astype(I32)
    smem = whole(pltpu.SMEM)
    hbm = whole(pl.ANY)

    request = call(request_kernel, held((DEVICES, 128), F32), [whole()])(cluster_lists)
    asked = exchange(request.reshape(DEVICES, 1, 128)).reshape(DEVICES, 128)
    empty = call(empty_kernel, shape((2, 8, PLACES), F32), [whole()])(cluster_lists)
    marks, rows, slots, early = call(
        expert_index_kernel,
        (
            shape((8, DEVICES), I32),
            shape((8, DEVICES), I32),
            shape((1, CHOSEN), I32),
            held((WIDTH, EARLY)),
        ),
        [smem, whole(), hbm],
        [pltpu.SemaphoreType.DMA(())],
    )(place, expert_lists, w_out)

    wanted, picked = call(
        select_kernel,
        (shape((3, SEQ, 128), F32), shape((DEVICES, 9, 8, HEAD))),
        [whole(), hbm],
        [pltpu.VMEM((3, ROWS, WIDTH), BF16), pltpu.SemaphoreType.DMA((1,))],
    )(near(asked), qkv.transpose(1, 0, 2))
    arrived = exchange(picked)

    outputs = call(
        attend_kernel,
        shape((DEVICES, 3, 8, HEAD)),
        [whole(), whole()],
        [
            pltpu.VMEM((2, 3, PLACES, HEAD), BF16),
            pltpu.VMEM((GROWS, GROWS), F32),
            pltpu.VMEM((GROWS, HEAD), BF16),
        ],
    )(empty, near(arrived))
    came_back = exchange(outputs)

    mixed, outgoing = call(
        mix_kernel,
        (shape((ROWS, WIDTH)), shape((SENT, CHUNKS, 128))),
        [hbm, hbm, whole(), whole(), hbm, hbm],
        [
            pltpu.SMEM((8, DEVICES), I32),
            pltpu.VMEM((3, SEQ, 128), F32),
            pltpu.VMEM((1, WIDTH), BF16),
            pltpu.VMEM((3, WIDTH, (WIDTH - EARLY) // 3), BF16),
            pltpu.VMEM((ROWS, WIDTH), BF16),
            pltpu.VMEM((ROWS * PITCH, 128), F32),
            pltpu.VMEM((ROWS, CHUNKS, 128), BF16),
            pltpu.SemaphoreType.DMA((3,)),
            pltpu.SemaphoreType.DMA((3,)),
        ],
    )(rows, wanted, near(came_back), near(early), w_out, norm_gain.reshape(1, WIDTH))
    incoming = exchange(outgoing)

    produced = call(
        expert_kernel,
        shape((SENT, CHUNKS, 128)),
        [hbm, hbm, whole(), hbm, hbm, hbm, hbm],
        [
            pltpu.SMEM((1,), I32),
            pltpu.SMEM((1, CHOSEN), I32),
            pltpu.VMEM((WIDTH, 128), BF16),
            pltpu.VMEM((SENT, CHUNKS, 128), BF16),
            pltpu.VMEM((3, WIDTH, HIDDEN // 3), BF16),
            pltpu.VMEM((3, WIDTH, HIDDEN // 3), BF16),
            pltpu.VMEM((HIDDEN, WIDTH), BF16),
            pltpu.VMEM((CHOSEN * PITCH, 128), F32),
            pltpu.VMEM((CHOSEN, WIDTH), BF16),
            pltpu.VMEM((CHOSEN, HIDDEN), BF16),
            pltpu.SemaphoreType.DMA((7,)),
            pltpu.SemaphoreType.DMA((4,)),
            pltpu.SemaphoreType.DMA((3,)),
        ],
        out_specs=hbm,
    )(place, slots, near(incoming), w_gate, w_up, w_down, router)
    results = exchange(produced)

    return call(
        combine_kernel,
        shape((ROWS, WIDTH)),
        [hbm, hbm, whole()],
        [
            pltpu.VMEM((SENT * PITCH, 128), F32),
            pltpu.VMEM((8, DEVICES), I32),
            pltpu.VMEM((ROWS, WIDTH), BF16),
            pltpu.SemaphoreType.DMA((2,)),
        ],
    )(marks, mixed, near(results))


def solution(mesh):
    return jax.shard_map(
        shards,
        mesh=mesh,
        in_specs=(
            P(("seq", "grp"), None, None),
            P("seq", "grp", None),
            P(),
            P(),
            P(),
            P(),
            P(("seq", "grp"), None, None),
            P(("seq", "grp"), None, None),
            P(("seq", "grp"), None, None),
        ),
        out_specs=P(("seq", "grp"), None),
        check_vma=False,
    )
```
